32 devices in a mesh: gx: 4 (over y, x), gy: 8 (over z, core).
Axes of the slice: x: 2, y: 2, z: 4, core: 2. Of those that a mesh axis runs over, the one named last changes fastest.
Arguments:
- adjoint_prev: float32 [2, 20, 256, 1024], P(None, None, 'gx', 'gy'), may hold values from -2 to 2
- viscosity: float32 [20, 256, 1024], P(None, 'gx', 'gy'), may hold values from 0.5 to 4
- friction: float32 [256, 1024], P('gx', 'gy'), may hold values from 0.5 to 20
- basal_velocity: float32 [2, 256, 1024], P(None, 'gx', 'gy'), may hold values from -6 to 6
- ice_mask: int32 [256, 1024], P('gx', 'gy'), may hold values 0 or 1
- misfit: bfloat16 [32768, 2, 128], P(('gx', 'gy')), may hold values from -60 to 60
- block_tile: int32 [32768, 1], P(('gx', 'gy')), may hold values from 0 to 31; in each aligned block of 1024 rows (0 to 1023, 1024 to 2047, ...) at most 64 rows name the same one
- block_row: int32 [32768], P(('gx', 'gy')), may hold values from 0 to 63
Outputs:
- adjoint: float32 [2, 20, 256, 1024], P(None, None, 'gx', 'gy')
- gradient: float32 [256, 1024], P('gx', 'gy')
The draws below stay inside these ranges and needn't reach their ends.
Inputs may be any that keep to these rules, and one draw needn't show every extreme that they name: `block_tile`: among the 1024 blocks of one device no tile is named more than 64 times, a bound that some block reaches.
All inputs are finite; a program needn't handle non-finite values. No bound on the sum of `ice_mask` on one device may be relied on, other than what follows from the above.
Results may differ from the reference program's by a relative error of at most 0.0003.
Values may be sent and summed in bfloat16 or wider, within the bound.
No kernel may reach another device: no remote copies, remote signals or barrier semaphores. Data moves between devices by JAX's collectives and lax.ppermute only.
A program may use at most 64 MiB of HBM per device.

```python
import math
import jax
import jax.numpy as jnp
import numpy as np

TX = 64
TY = 128
LAYERS = 20
ITERS = 3
SB = 1024
CAP = 64
NX = 256
NY = 1024
BLOCKS = 32768
N_GY = 8
DEVICES = 32


def with_ends(result, own_key, least, largest):
    extent = result.shape
    place = [jax.random.randint(jax.random.fold_in(own_key, axis), (), 0, extent[axis]) for axis in range(len(extent))]
    result = result.at[tuple(place)].set(least)
    longest = extent.index(max(extent))
    place[longest] = (place[longest] + 1) % extent[longest]
    return result.at[tuple(place)].set(largest)


def block_levels(rng, extent, shards, least, largest):
    loudness = 1.0
    for axis_at, shards_of in shards:
        draws = jax.random.uniform(jax.random.fold_in(jax.random.fold_in(rng, 6), axis_at), (shards_of,), jnp.float32, least / len(shards), largest / len(shards))
        loudness = loudness * jnp.repeat(jnp.exp(draws), extent[axis_at] // shards_of).reshape((-1,) + (1,) * (len(extent) - 1 - axis_at))
    return loudness


def routed_block(key, own, number, rows, amount, top, bound, skew):
    sequence = jax.random.permutation(key, amount)
    heavy_load, usual = load_shares(amount, rows * top, bound, skew, True), load_shares(amount, rows * top, bound, skew, False)
    places = jnp.arange(amount)

    def named(tallies, turn):
        used = int((tallies > 0).sum())
        fixed = max(1, used // 4)
        shifted = fixed + (places - fixed + turn * (used - fixed)) % max(1, amount - fixed)
        return jnp.zeros((amount,), jnp.int32).at[sequence[jnp.where(places < fixed, places, shifted)]].set(jnp.asarray(tallies, jnp.int32))

    tallies = jnp.where(number % 4 == 0, named(heavy_load, number // 4), named(usual, number - number // 4 - 1))
    mixed = jax.random.permutation(jax.random.fold_in(own, 3), amount)
    giver, sink = mixed[0:amount // 2 * 2:2], mixed[1:amount // 2 * 2:2]
    margin = jnp.minimum(tallies[giver] - 1, bound - tallies[sink]) // 2
    margin = jnp.where((giver == sequence[0]) | (sink == sequence[0]) | (tallies[sink] == 0), 0, jnp.maximum(margin, 0))
    shifted = jax.random.randint(jax.random.fold_in(own, 4), (amount // 2,), 0, 1 << 20) % (margin + 1)
    tallies = tallies.at[giver].add(-shifted).at[sink].add(shifted)
    labels = jnp.searchsorted(jnp.cumsum(tallies), jnp.arange(rows * top), side="right").astype(jnp.int32)
    listing = labels.reshape(top, rows).T
    listing = listing[jax.random.permutation(jax.random.fold_in(own, 1), rows)]
    turn = jax.random.randint(jax.random.fold_in(own, 2), (rows, 1), 0, top)
    return jnp.take_along_axis(listing, (jnp.arange(top)[None, :] + turn) % top, axis=1)


def load_shares(count, total, limit, lean, full):
    loads = [(1 << 20) // math.isqrt(grade ** lean) + 1 for grade in range(1, count + 1)]
    largest = limit if full else min(limit, max(-(-total // count), total * loads[0] // sum(loads)))
    least = 1 if total - largest >= count - 1 else 0
    counts, rest = [largest] + [least] * (count - 1), total - largest - least * (count - 1)
    while rest > 0:
        movable = [i for i in range(1, count) if counts[i] < largest] or [i for i in range(1, count) if counts[i] < limit]
        mass, budget = sum([loads[i] for i in movable]), rest
        for i in movable:
            more = min(limit - counts[i], max(1, budget * loads[i] // mass), rest)
            counts[i] = counts[i] + more
            rest = rest - more
    return np.array(counts)


def gaussian(key, shape, spread, bound, split=(), kind=jnp.bfloat16):
    entries = spread * jax.random.normal(key, shape, jnp.float32)
    if split:
        entries = entries * block_levels(key, shape, split, -0.22, 0.18)
    return jnp.clip(entries, -bound, bound).astype(kind)


def setup_inputs(seed: int = 0) -> dict:
    seeds = jax.random.split(jax.random.key(seed), 9)
    adjoint_prev = gaussian(seeds[0], (2, LAYERS, NX, NY), 0.3, 2.0, ((2, 4), (3, 8)), jnp.float32)
    viscosity = jnp.clip(jnp.exp(math.log(4.0) - 2.0794415 * jax.random.uniform(seeds[1], (LAYERS, NX, NY), jnp.float32) ** block_levels(seeds[1], (LAYERS, NX, NY), ((1, 4), (2, 8)), -0.2, 0.2)), 0.5, 4.0)
    friction = jnp.clip(jnp.exp(math.log(20.0) - 3.6888795 * jax.random.uniform(seeds[2], (NX, NY), jnp.float32) ** block_levels(seeds[2], (NX, NY), ((0, 4), (1, 8)), -0.2, 0.2)), 0.5, 20.0)
    basal_velocity = gaussian(seeds[3], (2, NX, NY), 1.0, 6.0, ((1, 4), (2, 8)), jnp.float32)
    ice_mask = with_ends((jax.random.randint(seeds[4], (NX, NY), 0, 4) < 3).astype(jnp.int32), jax.random.fold_in(seeds[4], 1), 0, 1)
    misfit = gaussian(seeds[5], (BLOCKS, 2, TY), 10.0, 60.0, ((0, 32),))
    block_tile_keys = jax.random.split(jax.random.fold_in(seeds[6], 1), BLOCKS // SB)
    block_tile_turns = jax.random.permutation(jax.random.fold_in(seeds[6], 3), BLOCKS // SB)
    block_tile = jax.vmap(lambda own, number: routed_block(jax.random.fold_in(seeds[6], 2), own, number, SB, DEVICES, 1, CAP, 2))(block_tile_keys, block_tile_turns).reshape((BLOCKS, 1))
    block_row = with_ends(jax.random.randint(seeds[7], (BLOCKS,), 0, TX), jax.random.fold_in(seeds[7], 1), 0, TX - 1).astype(jnp.int32)
    return dict(adjoint_prev=adjoint_prev, viscosity=viscosity, friction=friction, basal_velocity=basal_velocity, ice_mask=ice_mask, misfit=misfit, block_tile=block_tile, block_row=block_row)


VERTICAL = 4.0


def omega_list(count):
    return [1.0 / (1.3 + 1.2 * math.cos((2 * turn_id + 1) * math.pi / (2 * count))) for turn_id in range(count)]


def padded_of(values):
    widths = [(0, 0)] * (values.ndim - 2) + [(1, 1), (1, 1)]
    return jnp.pad(values, widths)


def coefficients(padded_eta, friction):
    center = padded_eta[:, 1:-1, 1:-1]
    x_low = 0.5 * (padded_eta[:, :-2, 1:-1] + center)
    x_high = 0.5 * (padded_eta[:, 2:, 1:-1] + center)
    y_low = 0.5 * (padded_eta[:, 1:-1, :-2] + center)
    y_high = 0.5 * (padded_eta[:, 1:-1, 2:] + center)
    layer_face = 0.5 * (center[:-1] + center[1:])
    zero_face = jnp.zeros_like(center[:1])
    z_up = jnp.concatenate([zero_face, layer_face], axis=0)
    z_down = jnp.concatenate([layer_face, zero_face], axis=0)
    basal = jnp.concatenate([jnp.zeros_like(center[:-1]), friction[None].astype(jnp.float32)], axis=0)
    horiz_x = x_low + x_high
    horiz_y = y_low + y_high
    vertical = VERTICAL * (z_up + z_down) + basal
    diagonal = jnp.stack([4.0 * horiz_x + horiz_y + vertical, horiz_x + 4.0 * horiz_y + vertical])
    return (x_low, x_high, y_low, y_high, z_up, z_down, basal), diagonal


def diffuse(padded, coeff, weight_x, weight_y):
    x_low, x_high, y_low, y_high, z_up, z_down, basal = coeff
    center = padded[:, 1:-1, 1:-1]
    zero_layer = jnp.zeros_like(center[:1])
    above = jnp.concatenate([zero_layer, center[:-1]], axis=0)
    below = jnp.concatenate([center[1:], zero_layer], axis=0)
    total = weight_x * (x_low * (center - padded[:, :-2, 1:-1]) + x_high * (center - padded[:, 2:, 1:-1]))
    total = total + weight_y * (y_low * (center - padded[:, 1:-1, :-2]) + y_high * (center - padded[:, 1:-1, 2:]))
    total = total + VERTICAL * (z_up * (center - above) + z_down * (center - below))
    return total + basal * center


def mixed(padded, padded_eta, weight_x, weight_y):
    along_y = 0.5 * (padded[:, :, 2:] - padded[:, :, :-2])
    flux_x = weight_x * padded_eta[:, :, 1:-1] * along_y
    along_x = 0.5 * (padded[:, 2:, :] - padded[:, :-2, :])
    flux_y = weight_y * padded_eta[:, 1:-1, :] * along_x
    return -(0.5 * (flux_x[:, 2:] - flux_x[:, :-2]) + 0.5 * (flux_y[:, :, 2:] - flux_y[:, :, :-2]))


def operate(padded_adj, padded_eta, coeff):
    first = diffuse(padded_adj[0], coeff, 4.0, 1.0) + mixed(padded_adj[1], padded_eta, 2.0, 1.0)
    second = diffuse(padded_adj[1], coeff, 1.0, 4.0) + mixed(padded_adj[0], padded_eta, 1.0, 2.0)
    return jnp.stack([first, second])


def reference(adjoint_prev, viscosity, friction, basal_velocity, ice_mask, misfit, block_tile, block_row):
    padded_eta = padded_of(viscosity)
    coeff, diagonal = coefficients(padded_eta, friction)
    ice = ice_mask.astype(jnp.float32)
    target = block_tile[:, 0].astype(jnp.int32)
    tile_x = target // N_GY
    tile_y = target % N_GY
    global_row = (tile_x * TX + block_row).astype(jnp.int32)
    values = jnp.transpose(misfit.astype(jnp.float32), (1, 0, 2))
    surface = jnp.zeros((2, NX, N_GY, TY), jnp.float32).at[:, global_row, tile_y, :].add(values)
    source = jnp.zeros((2, LAYERS, NX, NY), jnp.float32).at[:, 0].set(surface.reshape(2, NX, NY))
    adjoint = ice * adjoint_prev
    for omega in omega_list(ITERS):
        image = operate(padded_of(adjoint), padded_eta, coeff)
        adjoint = ice * (adjoint + omega * (source - image) / diagonal)
    gradient = -friction * ice * (basal_velocity[0] * adjoint[0, LAYERS - 1] + basal_velocity[1] * adjoint[1, LAYERS - 1])
    return adjoint, gradient
```

```python
import functools
import math

import jax
import jax.numpy as jnp
from jax import lax
from jax.experimental import pallas as pl
from jax.experimental.pallas import tpu as pltpu
from jax.sharding import PartitionSpec as P

ITERS = 3
HALO = ITERS
GROUP = 2 * HALO
PAD_UNITS = 4
VERTICAL = 4.0

F32 = jnp.float32
BF16 = jnp.bfloat16


def omega_list(count):
    return [
        1.0 / (1.3 + 1.2 * math.cos((2 * turn_id + 1) * math.pi / (2 * count)))
        for turn_id in range(count)
    ]


def shift_up(array, axis):
    peers = lax.axis_size(axis)
    return lax.ppermute(array, axis, [(i, i + 1) for i in range(peers - 1)])


def shift_down(array, axis):
    peers = lax.axis_size(axis)
    return lax.ppermute(array, axis, [(i + 1, i) for i in range(peers - 1)])


def vmem_specs(count):
    return [pl.BlockSpec(memory_space=pltpu.VMEM) for _ in range(count)]


def rows_before(values):
    return pltpu.roll(values, 1, 0)


def rows_after(values):
    return pltpu.roll(values, values.shape[0] - 1, 0)


def lanes_before(values, step=1):
    return pltpu.roll(values, step, 1)


def lanes_after(values, step=1):
    return pltpu.roll(values, values.shape[1] - step, 1)


def lane_index(shape):
    return lax.broadcasted_iota(jnp.int32, shape, len(shape) - 1)


def edge_kernel(layers, adj_lo, adj_hi, eta_lo, eta_hi, fr_lo, fr_hi, ice_lo, ice_hi, lo, hi):
    for adj, eta, fr, ice, out, at in (
        (adj_lo, eta_lo, fr_lo, ice_lo, lo, 0),
        (adj_hi, eta_hi, fr_hi, ice_hi, hi, 8 - HALO),
    ):
        rows = slice(at, at + HALO)
        covered = ice[rows, :] > 0
        for plane in range(2 * layers):
            values = jnp.where(covered, adj[plane // layers, plane % layers, rows, :], 0.0)
            out[HALO * plane : HALO * (plane + 1), :] = values
        for layer in range(layers):
            values = eta[layer, rows, :]
            first = HALO * (2 * layers + layer)
            out[first : first + HALO, :] = jnp.where(covered, values, -values)
        first = HALO * 3 * layers
        out[first : first + HALO, :] = fr[rows, :]


def edge_rows(adjoint, viscosity, friction, ice_mask):
    _, layers, rows, cols = adjoint.shape
    last = rows // 8 - 1
    length = -(-HALO * (3 * layers + 1) // 8) * 8

    def pair(block, index):
        return [
            pl.BlockSpec(block, functools.partial(index, 0)),
            pl.BlockSpec(block, functools.partial(index, last)),
        ]

    specs = pair((2, layers, 8, cols), lambda r, i: (0, 0, r, 0))
    specs += pair((layers, 8, cols), lambda r, i: (0, r, 0))
    specs += pair((8, cols), lambda r, i: (r, 0))
    specs += pair((8, cols), lambda r, i: (r, 0))
    return pl.pallas_call(
        functools.partial(edge_kernel, layers),
        grid=(1,),
        in_specs=specs,
        out_specs=[pl.BlockSpec((length, cols), lambda i: (0, 0))] * 2,
        out_shape=[jax.ShapeDtypeStruct((length, cols), F32)] * 2,
        name="edge_rows",
    )(adjoint, adjoint, viscosity, viscosity, friction, friction, ice_mask, ice_mask)


def column_kernel(layers, adj, eta, fr, ice, above, below, u_out, v_out, e_out, f_out, packed):
    rows, cols = fr.shape
    circle = rows + 8
    lane_layer = lane_index((circle, cols)) // GROUP
    covered = ice[...] > 0
    gap = jnp.zeros((8 - 2 * HALO, cols), F32)

    def extend(out, values, plane):
        first = HALO * plane
        out[:rows, :] = values
        out[rows : rows + HALO, :] = below[first : first + HALO, :]
        out[rows + HALO : circle - HALO, :] = gap
        out[circle - HALO : circle, :] = above[first : first + HALO, :]

    def gather(total, values, layer):
        return jnp.where(
            lane_layer == layer, pltpu.roll(values, (HALO + GROUP * layer) % cols, 1), total
        )

    totals = [jnp.zeros((circle, cols), F32)] * 3
    for layer in range(layers):
        extend(u_out.at[layer], jnp.where(covered, adj[0, layer], 0.0), layer)
        extend(v_out.at[layer], jnp.where(covered, adj[1, layer], 0.0), layers + layer)
        values = eta[layer]
        extend(e_out.at[layer], jnp.where(covered, values, -values), 2 * layers + layer)
        for field, out in enumerate((u_out, v_out, e_out)):
            totals[field] = gather(totals[field], out[layer], layer)
    extend(f_out, fr[...], 3 * layers)
    totals[2] = gather(totals[2], f_out[...], layers)
    for field in range(3):
        packed[field] = totals[field]


def edge_columns(adjoint, viscosity, friction, ice_mask, above, below):
    _, layers, rows, cols = adjoint.shape
    circle = rows + 8
    field = jax.ShapeDtypeStruct((layers, circle, cols), F32)
    return pl.pallas_call(
        functools.partial(column_kernel, layers),
        in_specs=vmem_specs(6),
        out_specs=vmem_specs(5),
        out_shape=[
            field,
            field,
            field,
            jax.ShapeDtypeStruct((circle, cols), F32),
            jax.ShapeDtypeStruct((3, circle, cols), F32),
        ],
        name="edge_columns",
    )(adjoint, viscosity, friction, ice_mask, above, below)


def strip_step(eta, scale, fields, omega, sources=None):
    parts = []
    for f in fields:
        p = eta * f
        y_low, y_high = lanes_before(f), lanes_after(f)
        x_low, x_high = rows_before(f), rows_after(f)
        parts.append(
            dict(
                p=p,
                sum_x=x_low + x_high,
                sum_y=y_low + y_high,
                sum_z=lanes_before(f, GROUP) + lanes_after(f, GROUP),
                p_z=lanes_before(p, GROUP) + lanes_after(p, GROUP),
                g=eta * (y_high - y_low),
                h=eta * (x_high - x_low),
            )
        )
    news, lows, highs = [], [], []
    for c in range(2):
        mine, other = parts[c], parts[1 - c]
        wg, wh = (0.25, 0.5) if c == 0 else (0.5, 0.25)
        cross_x, cross_y = wg * other["g"], wh * other["h"]
        low, high = mine["p"] - cross_y, mine["p"] + cross_y
        lows.append(low)
        highs.append(high)
        if omega is None:
            continue
        along_x = rows_after(mine["p"] + cross_x) + rows_before(mine["p"] - cross_x)
        along_y = lanes_after(high) + lanes_before(low)
        if c == 0:
            near = mine["sum_x"] + mine["sum_z"] + 0.25 * mine["sum_y"]
            rest = along_x + mine["p_z"] + 0.25 * along_y
        else:
            near = mine["sum_y"] + mine["sum_z"] + 0.25 * mine["sum_x"]
            rest = along_y + mine["p_z"] + 0.25 * along_x
        total = eta * near + rest
        if sources is not None:
            total = total + 0.5 * sources[c]
        news.append((1.0 - omega) * fields[c] + omega * (scale[c] * total))
    return news, lows, highs


def joined(left, right, column):
    return jnp.where(column == HALO - 1, left, right)


def plane_step(k, lane, eta, fields, products, scale, edges, sums, omega, source=None):
    shift = GROUP * k + HALO
    shape = lane.shape
    back = shape[1] - shift
    first, last = lane == 0, lane == shape[1] - 1
    e = eta[k + 1]
    parts = []
    for c in range(2):
        f = fields[c, k + 1]
        edge = pltpu.roll(edges[c], back, 1)
        y_low = lanes_before(jnp.where(last, edge, f))
        y_high = lanes_after(jnp.where(first, edge, f))
        x_low, x_high = rows_before(f), rows_after(f)
        parts.append(
            dict(
                f=f,
                p=products[c, k + 1],
                sum_x=x_low + x_high,
                sum_y=y_low + y_high,
                g=e * (y_high - y_low),
                h=e * (x_high - x_low),
            )
        )
    news = []
    for c in range(2):
        mine, other = parts[c], parts[1 - c]
        wg, wh = (0.25, 0.5) if c == 0 else (0.5, 0.25)
        cross_x, cross_y = wg * other["g"], wh * other["h"]
        p = mine["p"]
        edge = pltpu.roll(sums[c], back, 1)
        along_x = rows_after(p + cross_x) + rows_before(p - cross_x)
        along_y = lanes_after(jnp.where(first, edge, p + cross_y))
        along_y = along_y + lanes_before(jnp.where(last, edge, p - cross_y))
        sum_z = fields[c, k] + fields[c, k + 2]
        p_z = products[c, k] + products[c, k + 2]
        if c == 0:
            near = mine["sum_x"] + sum_z + 0.25 * mine["sum_y"]
            rest = along_x + p_z + 0.25 * along_y
        else:
            near = mine["sum_y"] + sum_z + 0.25 * mine["sum_x"]
            rest = along_y + p_z + 0.25 * along_x
        total = e * near + rest
        if source is not None:
            total = total + source[c]
        news.append((1.0 - omega) * mine["f"] + omega * (scale[c, k] * total))
    return news


def inverse_pair(e, e_x, e_y, e_z, ends, basal, covered):
    vertical = (VERTICAL / 2) * (e_z + ends * e) + basal
    both_x, both_y = e_x + 2.0 * e, e_y + 2.0 * e
    out = []
    for wx, wy in ((2.0, 0.5), (0.5, 2.0)):
        diagonal = wx * both_x + wy * both_y + vertical
        safe = jnp.where(covered, diagonal, 1.0)
        out.append(jnp.where(covered, 2.0 / safe, 0.0))
    return out


def sweep_kernel(
    layers,
    u_in, v_in, e_in, f_in, packed, packed_left, packed_right, basal_velocity,
    out, gradient, scale_out, eta_out, strip_out,
    fields, products, eta, scale, edges, sums,
):
    circle, cols = f_in.shape
    rows = out.shape[2]
    lane = lane_index((circle, cols))
    column = lane % GROUP
    omegas = omega_list(ITERS)
    zero = jnp.zeros((circle, cols), F32)

    strips = []
    for side in range(2):
        values = []
        for field in range(3):
            own = packed[field]
            if side == 0:
                values.append(jnp.where(column < HALO, packed_left[field], own))
            else:
                values.append(jnp.where(column < HALO, own, packed_right[field]))
        signed = values[2]
        inside = lane < GROUP * layers
        bottom = inside & (lane >= GROUP * (layers - 1))
        covered = inside & (signed > 0.0)
        e = jnp.where(inside, jnp.abs(signed), 0.0)
        basal = jnp.where(bottom, lanes_after(signed, GROUP), 0.0)
        ends = jnp.where(bottom | (lane < GROUP), 1.0, 2.0)
        pair = inverse_pair(
            e,
            rows_before(e) + rows_after(e),
            lanes_before(e) + lanes_after(e),
            lanes_before(e, GROUP) + lanes_after(e, GROUP),
            ends,
            basal,
            covered,
        )
        strip_out[side, 0] = e
        strip_out[side, 1] = pair[0]
        strip_out[side, 2] = pair[1]
        strips.append((e, pair, values[:2]))
    eta_edge = joined(strips[0][0], strips[1][0], column)
    states = [strips[0][2], strips[1][2]]
    for turn, omega in enumerate(omegas):
        step = omega if turn < ITERS - 1 else None
        left, lows, _ = strip_step(strips[0][0], strips[0][1], states[0], step)
        right, _, highs = strip_step(strips[1][0], strips[1][1], states[1], step)
        for c in range(2):
            edges[turn, c] = joined(states[0][c], states[1][c], column)
            sums[turn, c] = joined(lows[c], highs[c], column)
        states = [left, right]

    for stack in (eta, fields.at[0, 0], fields.at[0, 1], fields.at[1, 0], fields.at[1, 1]):
        stack[0] = zero
        stack[layers + 1] = zero
    for half in range(2):
        for c in range(2):
            products[half, c, 0] = zero
            products[half, c, layers + 1] = zero

    def load(k, carry):
        e = jnp.abs(e_in[k])
        eta[k + 1] = e
        for c, values in enumerate((u_in, v_in)):
            f = values[k]
            fields[0, c, k + 1] = f
            products[0, c, k + 1] = e * f
        return carry

    lax.fori_loop(0, layers, load, 0)

    def weigh(k, carry):
        e = eta[k + 1]
        edge = pltpu.roll(eta_edge, cols - (GROUP * k + HALO), 1)
        e_y = lanes_before(jnp.where(lane == cols - 1, edge, e))
        e_y = e_y + lanes_after(jnp.where(lane == 0, edge, e))
        is_end = (k == 0) | (k == layers - 1)
        ends = jnp.where(is_end, 1.0, 2.0)
        basal = jnp.where(k == layers - 1, 1.0, 0.0) * f_in[...]
        pair = inverse_pair(
            e,
            rows_before(e) + rows_after(e),
            e_y,
            eta[k] + eta[k + 2],
            ends,
            basal,
            e_in[k] > 0.0,
        )
        scale[0, k] = pair[0]
        scale[1, k] = pair[1]
        return carry

    lax.fori_loop(0, layers, weigh, 0)

    for turn, omega in enumerate(omegas):
        half, final = turn % 2, turn == ITERS - 1
        near = (edges.at[turn], sums.at[turn])

        def sweep(k, carry, half=half, final=final, near=near, omega=omega):
            pair = plane_step(
                k, lane, eta, fields.at[half], products.at[half], scale,
                (near[0][0], near[0][1]), (near[1][0], near[1][1]), omega,
            )
            for c in range(2):
                if final:
                    out[c, k] = pair[c][:rows]
                else:
                    fields[1 - half, c, k + 1] = pair[c]
                    products[1 - half, c, k + 1] = eta[k + 1] * pair[c]
            return carry

        lax.fori_loop(0, layers, sweep, 0)

    covered = e_in[layers - 1][:rows] > 0.0
    flow = basal_velocity[0] * out[0, layers - 1] + basal_velocity[1] * out[1, layers - 1]
    gradient[...] = jnp.where(covered, -f_in[...][:rows] * flow, 0.0)
    for k in range(ITERS):
        for c in range(2):
            scale_out[c, k] = scale[c, k]
    for k in range(ITERS + 1):
        eta_out[k] = eta[k + 1]


def free_sweeps(u, v, e, f, packed, left, right, basal_velocity):
    layers, circle, cols = u.shape
    rows = basal_velocity.shape[1]
    plane = (circle, cols)
    stack = (layers + 2,) + plane
    return pl.pallas_call(
        functools.partial(sweep_kernel, layers),
        in_specs=vmem_specs(8),
        out_specs=vmem_specs(5),
        out_shape=[
            jax.ShapeDtypeStruct((2, layers, rows, cols), F32),
            jax.ShapeDtypeStruct((rows, cols), F32),
            jax.ShapeDtypeStruct((2, ITERS) + plane, F32),
            jax.ShapeDtypeStruct((ITERS + 1,) + plane, F32),
            jax.ShapeDtypeStruct((2, 3) + plane, F32),
        ],
        scratch_shapes=[
            pltpu.VMEM((2, 2) + stack, F32),
            pltpu.VMEM((2, 2) + stack, F32),
            pltpu.VMEM(stack, F32),
            pltpu.VMEM((2, layers) + plane, F32),
            pltpu.VMEM((ITERS, 2) + plane, F32),
            pltpu.VMEM((ITERS, 2) + plane, F32),
        ],
        cost_estimate=pl.CostEstimate(
            flops=200_000_000, transcendentals=0, bytes_accessed=8_000_000
        ),
        name="free_sweeps",
    )(u, v, e, f, packed, left, right, basal_velocity)


def pack_kernel(devices, capacity, units, tile, row, misfit, out, slot_vector, slot, sem):
    turns, lanes = tile.shape
    device = lax.broadcasted_iota(jnp.int32, (devices, lanes), 0)
    at_row = lax.broadcasted_iota(jnp.int32, (lanes, lanes), 0)
    at_lane = lax.broadcasted_iota(jnp.int32, (lanes, lanes), 1)
    earlier = jnp.where(at_row < at_lane, 1.0, 0.0).astype(BF16)
    seen = jnp.zeros((devices, 1), F32)
    keys = jnp.zeros((devices, lanes), F32)
    for turn in range(turns):
        target = tile[turn : turn + 1, :]
        onehot = jnp.where(device == target, 1.0, 0.0)
        before = jnp.dot(onehot.astype(BF16), earlier, preferred_element_type=F32) + seen
        rank = jnp.sum(onehot * before, axis=0, keepdims=True).astype(jnp.int32)
        slot_vector[turn : turn + 1, :] = target * units + rank
        seen = seen + jnp.sum(onehot, axis=1, keepdims=True)
        named = onehot * (row[turn : turn + 1, :] + 1).astype(F32)
        place = jnp.where(at_row // 2 == rank, 1.0, 0.0).astype(BF16)
        keys = keys + lax.dot_general(
            named.astype(BF16), place, (((1,), (1,)), ((), ())), preferred_element_type=F32
        )
    copy = pltpu.make_async_copy(slot_vector, slot, sem)
    copy.start()
    out[...] = jnp.zeros(out.shape, BF16)
    upper = lax.broadcasted_iota(jnp.int32, (2, lanes), 0) == 0
    for d in range(devices):
        both = jnp.where(upper, jnp.broadcast_to(keys[d : d + 1, :], (2, lanes)), 0.0)
        out[d * units + capacity] = both.astype(BF16)
    copy.wait()

    def place_row(turn, carry):
        for i in range(lanes):
            out[slot[turn, i]] = misfit[turn * lanes + i]
        return carry

    lax.fori_loop(0, turns, place_row, 0)


def pack_blocks(misfit, block_tile, block_row, devices):
    count, _, cols = misfit.shape
    capacity = 2 * count // devices
    units = capacity + PAD_UNITS
    grid_shape = (count // cols, cols)
    packed = pl.pallas_call(
        functools.partial(pack_kernel, devices, capacity, units),
        in_specs=vmem_specs(3),
        out_specs=pl.BlockSpec(memory_space=pltpu.VMEM),
        out_shape=jax.ShapeDtypeStruct((devices * units, 2, cols), BF16),
        scratch_shapes=[
            pltpu.VMEM(grid_shape, jnp.int32),
            pltpu.SMEM(grid_shape, jnp.int32),
            pltpu.SemaphoreType.DMA,
        ],
        name="pack_blocks",
    )(block_tile.reshape(grid_shape), block_row.reshape(grid_shape), misfit)
    return packed.reshape(devices * units * 2, cols)


def surface_kernel(devices, capacity, units, got, surface, low, high):
    rows, lanes = surface.shape[1:]
    span = 2 * capacity
    group = max(1, lanes // span)
    at_row = lax.broadcasted_iota(jnp.int32, (2 * rows, lanes), 0).astype(F32)
    odd = (lax.broadcasted_iota(jnp.int32, (1, lanes), 1) % 2).astype(F32) * rows
    total = jnp.zeros((2 * rows, lanes), F32)
    for first in range(0, devices, group):
        key = None
        values = []
        for q in range(group):
            start = (first + q) * units * 2
            tile = got[start + span : start + span + 8, :].astype(F32)[:1, :]
            tile = pltpu.roll(tile, q * span, 1) if q else tile
            key = tile if key is None else key + tile
            values.append(got[start : start + span, :])
        wanted = jnp.where(key > 0.0, key - 1.0 + odd, -1.0)
        select = jnp.where(at_row == wanted, 1.0, 0.0).astype(BF16)
        block = values[0] if group == 1 else jnp.concatenate(values, axis=0)
        total = total + jnp.dot(select, block, preferred_element_type=F32)
    for c in range(2):
        surface[c] = total[c * rows : (c + 1) * rows]
    low[...] = jnp.zeros(low.shape, F32)
    high[...] = jnp.zeros(high.shape, F32)
    for c in range(2):
        low[2 * c : 2 * c + 2, :] = surface[c, :2, :]
        high[2 * c : 2 * c + 2, :] = surface[c, rows - 2 :, :]


def sum_blocks(got, devices, capacity, rows):
    cols = got.shape[1]
    edge = jax.ShapeDtypeStruct((8, cols), F32)
    return pl.pallas_call(
        functools.partial(surface_kernel, devices, capacity, capacity + PAD_UNITS),
        in_specs=vmem_specs(1),
        out_specs=vmem_specs(3),
        out_shape=[jax.ShapeDtypeStruct((2, rows, cols), F32), edge, edge],
        name="sum_blocks",
    )(got)


def source_kernel(surface, above, below, source, packed):
    rows, cols = surface.shape[1:]
    circle = rows + 8
    for c in range(2):
        source[c, :rows, :] = surface[c]
        source[c, rows : rows + 2, :] = below[2 * c : 2 * c + 2, :]
        source[c, rows + 2 : circle - 2, :] = jnp.zeros((4, cols), F32)
        source[c, circle - 2 : circle, :] = above[2 * c : 2 * c + 2, :]
    lane = lane_index((circle, cols))
    first = jnp.where(lane < GROUP, lanes_before(source[0], HALO), 0.0)
    both = jnp.where(lane // GROUP == 1, lanes_before(source[1], HALO + GROUP), first)
    packed[...] = both


def source_columns(surface, above, below):
    _, rows, cols = surface.shape
    circle = rows + 8
    return pl.pallas_call(
        source_kernel,
        in_specs=vmem_specs(3),
        out_specs=vmem_specs(2),
        out_shape=[
            jax.ShapeDtypeStruct((2, circle, cols), F32),
            jax.ShapeDtypeStruct((circle, cols), F32),
        ],
        name="source_columns",
    )(surface, above, below)


def response_kernel(
    source, packed, packed_left, packed_right, scale, eta_in, strip_in, adj_in,
    out, fields, products, eta,
):
    circle, cols = packed.shape
    rows = out.shape[2]
    lane = lane_index((circle, cols))
    column = lane % GROUP
    omegas = omega_list(ITERS)
    zero = jnp.zeros((circle, cols), F32)
    top = lane < GROUP

    strips = []
    for side in range(2):
        if side == 0:
            both = jnp.where(column < HALO, packed_left[...], packed[...])
        else:
            both = jnp.where(column < HALO, packed[...], packed_right[...])
        pair = (jnp.where(top, both, 0.0), jnp.where(top, lanes_after(both, GROUP), 0.0))
        strips.append((strip_in[side, 0], (strip_in[side, 1], strip_in[side, 2]), pair))
    states = [
        [(0.5 * omegas[0]) * (weight[c] * pair[c]) for c in range(2)] for _, weight, pair in strips
    ]
    near = []
    for turn in range(1, ITERS):
        omega = omegas[turn] if turn < ITERS - 1 else None
        left, lows, _ = strip_step(strips[0][0], strips[0][1], states[0], omega, strips[0][2])
        right, _, highs = strip_step(strips[1][0], strips[1][1], states[1], omega, strips[1][2])
        near.append(
            (
                [joined(states[0][c], states[1][c], column) for c in range(2)],
                [joined(lows[c], highs[c], column) for c in range(2)],
            )
        )
        states = [left, right]

    eta[0] = zero
    for k in range(ITERS + 1):
        eta[k + 1] = eta_in[k]
    for half in range(2):
        for c in range(2):
            for k in range(ITERS + 2):
                fields[half, c, k] = zero
                products[half, c, k] = zero
    drive = [0.5 * source[c] for c in range(2)]
    for c in range(2):
        f = omegas[0] * (scale[c, 0] * drive[c])
        fields[0, c, 1] = f
        products[0, c, 1] = eta[1] * f
    for turn in range(1, ITERS):
        half, final = (turn - 1) % 2, turn == ITERS - 1
        edges, sums = near[turn - 1]
        for k in range(turn + 1):
            pair = plane_step(
                k, lane, eta, fields.at[half], products.at[half], scale, edges, sums,
                omegas[turn], drive if k == 0 else None,
            )
            for c in range(2):
                if final:
                    out[c, k] = adj_in[c, k] + pair[c][:rows]
                else:
                    fields[1 - half, c, k + 1] = pair[c]
                    products[1 - half, c, k + 1] = eta[k + 1] * pair[c]


def add_response(source, packed, left, right, scale, eta, strips, adjoint):
    circle, cols = packed.shape
    _, layers, rows, _ = adjoint.shape
    plane = (circle, cols)
    top = pl.BlockSpec((2, ITERS, rows, cols), lambda i: (0, 0, 0, 0))

    def whole(array):
        return pl.BlockSpec(array.shape, lambda i, n=array.ndim: (0,) * n)

    operands = (source, packed, left, right, scale, eta, strips)
    return pl.pallas_call(
        response_kernel,
        grid=(1,),
        in_specs=[whole(array) for array in operands] + [top],
        out_specs=top,
        out_shape=jax.ShapeDtypeStruct(adjoint.shape, F32),
        scratch_shapes=[
            pltpu.VMEM((2, 2, ITERS + 2) + plane, F32),
            pltpu.VMEM((2, 2, ITERS + 2) + plane, F32),
            pltpu.VMEM((ITERS + 2,) + plane, F32),
        ],
        input_output_aliases={7: 0},
        name="add_response",
    )(*operands, adjoint)


def on_device(
    adjoint_prev, viscosity, friction, basal_velocity, ice_mask, misfit, block_tile, block_row
):
    devices = lax.axis_size("gx") * lax.axis_size("gy")
    layers, rows, cols = adjoint_prev.shape[1:]
    capacity = 2 * misfit.shape[0] // devices
    assert layers > 2 * ITERS and GROUP * (layers + 1) <= cols and rows % 8 == 0
    assert 2 * capacity <= cols and cols % (2 * capacity) == 0 and misfit.shape[0] % cols == 0

    edge_low, edge_high = edge_rows(adjoint_prev, viscosity, friction, ice_mask)
    above = shift_up(edge_high, "gx")
    below = shift_down(edge_low, "gx")
    sent = pack_blocks(misfit, block_tile, block_row, devices)
    got = lax.all_to_all(
        sent.reshape(devices, -1, cols), ("gx", "gy"), split_axis=0, concat_axis=0, tiled=True
    )
    u, v, e, f, packed = edge_columns(
        adjoint_prev, viscosity, friction, ice_mask, above, below
    )
    left = shift_up(packed, "gy")
    right = shift_down(packed, "gy")
    adjoint, gradient, scale, eta, strips = free_sweeps(
        u, v, e, f, packed, left, right, basal_velocity
    )
    surface, low, high = sum_blocks(got.reshape(-1, cols), devices, capacity, rows)
    source, source_packed = source_columns(
        surface, shift_up(high, "gx"), shift_down(low, "gx")
    )
    source_left = shift_up(source_packed, "gy")
    source_right = shift_down(source_packed, "gy")
    adjoint = add_response(
        source, source_packed, source_left, source_right, scale, eta, strips, adjoint
    )
    return (adjoint, gradient)


def solution(mesh):
    placed = (
        P(None, None, "gx", "gy"),
        P(None, "gx", "gy"),
        P("gx", "gy"),
        P(None, "gx", "gy"),
        P("gx", "gy"),
        P(("gx", "gy"), None, None),
        P(("gx", "gy"), None),
        P(("gx", "gy")),
    )
    return jax.shard_map(
        on_device,
        mesh=mesh,
        in_specs=placed,
        out_specs=(P(None, None, "gx", "gy"), P("gx", "gy")),
        check_vma=False,
    )
```

```python
import functools
import math

import jax
import jax.numpy as jnp
from jax import lax
from jax.experimental import pallas as pl
from jax.experimental.pallas import tpu as pltpu
from jax.sharding import PartitionSpec as P


ITERS = 3
HALO = ITERS
GROUP = 2 * HALO
PAD_UNITS = 4
VERTICAL = 4.0

F32 = jnp.float32
BF16 = jnp.bfloat16


def omega_list(count):
    return [
        1.0 / (1.3 + 1.2 * math.cos((2 * turn_id + 1) * math.pi / (2 * count)))
        for turn_id in range(count)
    ]


def shift_up(array, axis):
    peers = lax.axis_size(axis)
    return lax.ppermute(array, axis, [(i, i + 1) for i in range(peers - 1)])


def shift_down(array, axis):
    peers = lax.axis_size(axis)
    return lax.ppermute(array, axis, [(i + 1, i) for i in range(peers - 1)])


def vmem_specs(count):
    return [pl.BlockSpec(memory_space=pltpu.VMEM) for _ in range(count)]


def rows_before(values):
    return pltpu.roll(values, 1, 0)


def rows_after(values):
    return pltpu.roll(values, values.shape[0] - 1, 0)


def lanes_before(values, step=1):
    return pltpu.roll(values, step, 1)


def lanes_after(values, step=1):
    return pltpu.roll(values, values.shape[1] - step, 1)


def lane_index(shape):
    return lax.broadcasted_iota(jnp.int32, shape, len(shape) - 1)


def edge_kernel(layers, adj_lo, adj_hi, eta_lo, eta_hi, fr_lo, fr_hi, ice_lo, ice_hi, lo, hi):
    for adj, eta, fr, ice, out, at in (
        (adj_lo, eta_lo, fr_lo, ice_lo, lo, 0),
        (adj_hi, eta_hi, fr_hi, ice_hi, hi, 8 - HALO),
    ):
        rows = slice(at, at + HALO)
        covered = ice[rows, :] > 0
        for plane in range(2 * layers):
            values = jnp.where(covered, adj[plane // layers, plane % layers, rows, :], 0.0)
            out[HALO * plane : HALO * (plane + 1), :] = values
        for layer in range(layers):
            values = eta[layer, rows, :]
            first = HALO * (2 * layers + layer)
            out[first : first + HALO, :] = jnp.where(covered, values, -values)
        first = HALO * 3 * layers
        out[first : first + HALO, :] = fr[rows, :]


def edge_rows(adjoint, viscosity, friction, ice_mask):
    _, layers, rows, cols = adjoint.shape
    last = rows // 8 - 1
    length = -(-HALO * (3 * layers + 1) // 8) * 8

    def pair(block, index):
        return [
            pl.BlockSpec(block, functools.partial(index, 0)),
            pl.BlockSpec(block, functools.partial(index, last)),
        ]

    specs = pair((2, layers, 8, cols), lambda r, i: (0, 0, r, 0))
    specs += pair((layers, 8, cols), lambda r, i: (0, r, 0))
    specs += pair((8, cols), lambda r, i: (r, 0))
    specs += pair((8, cols), lambda r, i: (r, 0))
    return pl.pallas_call(
        functools.partial(edge_kernel, layers),
        grid=(1,),
        in_specs=specs,
        out_specs=[pl.BlockSpec((length, cols), lambda i: (0, 0))] * 2,
        out_shape=[jax.ShapeDtypeStruct((length, cols), F32)] * 2,
        compiler_params=pltpu.CompilerParams(vmem_limit_bytes=4 << 20),
        name="edge_rows",
    )(adjoint, adjoint, viscosity, viscosity, friction, friction, ice_mask, ice_mask)


def column_kernel(layers, adj, eta, fr, ice, above, below, u_out, v_out, e_out, f_out, packed):
    rows, cols = fr.shape
    circle = rows + 8
    lane_layer = lane_index((circle, cols)) // GROUP
    covered = ice[...] > 0
    gap = jnp.zeros((8 - 2 * HALO, cols), F32)

    def extend(out, values, plane):
        first = HALO * plane
        out[:rows, :] = values
        out[rows : rows + HALO, :] = below[first : first + HALO, :]
        out[rows + HALO : circle - HALO, :] = gap
        out[circle - HALO : circle, :] = above[first : first + HALO, :]

    def gather(total, values, layer):
        return jnp.where(
            lane_layer == layer, pltpu.roll(values, (HALO + GROUP * layer) % cols, 1), total
        )

    totals = [jnp.zeros((circle, cols), F32)] * 3
    for layer in range(layers):
        extend(u_out.at[layer], jnp.where(covered, adj[0, layer], 0.0), layer)
        extend(v_out.at[layer], jnp.where(covered, adj[1, layer], 0.0), layers + layer)
        values = eta[layer]
        extend(e_out.at[layer], jnp.where(covered, values, -values), 2 * layers + layer)
        for field, out in enumerate((u_out, v_out, e_out)):
            totals[field] = gather(totals[field], out[layer], layer)
    extend(f_out, fr[...], 3 * layers)
    totals[2] = gather(totals[2], f_out[...], layers)
    for field in range(3):
        packed[field] = totals[field]


def edge_columns(adjoint, viscosity, friction, ice_mask, above, below):
    _, layers, rows, cols = adjoint.shape
    circle = rows + 8
    field = jax.ShapeDtypeStruct((layers, circle, cols), F32)
    return pl.pallas_call(
        functools.partial(column_kernel, layers),
        in_specs=vmem_specs(6),
        out_specs=vmem_specs(5),
        out_shape=[
            field,
            field,
            field,
            jax.ShapeDtypeStruct((circle, cols), F32),
            jax.ShapeDtypeStruct((3, circle, cols), F32),
        ],
        compiler_params=pltpu.CompilerParams(vmem_limit_bytes=12 << 20),
        name="edge_columns",
    )(adjoint, viscosity, friction, ice_mask, above, below)


def strip_step(eta, scale, fields, omega, sources=None):
    parts = []
    for f in fields:
        p = eta * f
        y_low, y_high = lanes_before(f), lanes_after(f)
        x_low, x_high = rows_before(f), rows_after(f)
        parts.append(
            dict(
                p=p,
                sum_x=x_low + x_high,
                sum_y=y_low + y_high,
                sum_z=lanes_before(f, GROUP) + lanes_after(f, GROUP),
                p_z=lanes_before(p, GROUP) + lanes_after(p, GROUP),
                g=eta * (y_high - y_low),
                h=eta * (x_high - x_low),
            )
        )
    news, lows, highs = [], [], []
    for c in range(2):
        mine, other = parts[c], parts[1 - c]
        wg, wh = (0.25, 0.5) if c == 0 else (0.5, 0.25)
        cross_x, cross_y = wg * other["g"], wh * other["h"]
        low, high = mine["p"] - cross_y, mine["p"] + cross_y
        lows.append(low)
        highs.append(high)
        if omega is None:
            continue
        along_x = rows_after(mine["p"] + cross_x) + rows_before(mine["p"] - cross_x)
        along_y = lanes_after(high) + lanes_before(low)
        if c == 0:
            near = mine["sum_x"] + mine["sum_z"] + 0.25 * mine["sum_y"]
            rest = along_x + mine["p_z"] + 0.25 * along_y
        else:
            near = mine["sum_y"] + mine["sum_z"] + 0.25 * mine["sum_x"]
            rest = along_y + mine["p_z"] + 0.25 * along_x
        total = eta * near + rest
        if sources is not None:
            total = total + 0.5 * sources[c]
        news.append((1.0 - omega) * fields[c] + omega * (scale[c] * total))
    return news, lows, highs


def joined(left, right, column):
    return jnp.where(column == HALO - 1, left, right)


def plane_step(k, lane, eta, fields, products, scale, edges, sums, omega, source=None):
    shift = GROUP * k + HALO
    shape = lane.shape
    back = shape[1] - shift
    first, last = lane == 0, lane == shape[1] - 1
    e = eta[k + 1]
    parts = []
    for c in range(2):
        f = fields[c, k + 1]
        edge = pltpu.roll(edges[c], back, 1)
        y_low = lanes_before(jnp.where(last, edge, f))
        y_high = lanes_after(jnp.where(first, edge, f))
        x_low, x_high = rows_before(f), rows_after(f)
        parts.append(
            dict(
                f=f,
                p=products[c, k + 1],
                sum_x=x_low + x_high,
                sum_y=y_low + y_high,
                g=e * (y_high - y_low),
                h=e * (x_high - x_low),
            )
        )
    news = []
    for c in range(2):
        mine, other = parts[c], parts[1 - c]
        wg, wh = (0.25, 0.5) if c == 0 else (0.5, 0.25)
        cross_x, cross_y = wg * other["g"], wh * other["h"]
        p = mine["p"]
        edge = pltpu.roll(sums[c], back, 1)
        along_x = rows_after(p + cross_x) + rows_before(p - cross_x)
        along_y = lanes_after(jnp.where(first, edge, p + cross_y))
        along_y = along_y + lanes_before(jnp.where(last, edge, p - cross_y))
        sum_z = fields[c, k] + fields[c, k + 2]
        p_z = products[c, k] + products[c, k + 2]
        if c == 0:
            near = mine["sum_x"] + sum_z + 0.25 * mine["sum_y"]
            rest = along_x + p_z + 0.25 * along_y
        else:
            near = mine["sum_y"] + sum_z + 0.25 * mine["sum_x"]
            rest = along_y + p_z + 0.25 * along_x
        total = e * near + rest
        if source is not None:
            total = total + source[c]
        news.append((1.0 - omega) * mine["f"] + omega * (scale[c, k] * total))
    return news


def inverse_pair(e, e_x, e_y, e_z, ends, basal, covered):
    vertical = (VERTICAL / 2) * (e_z + ends * e) + basal
    both_x, both_y = e_x + 2.0 * e, e_y + 2.0 * e
    out = []
    for wx, wy in ((2.0, 0.5), (0.5, 2.0)):
        diagonal = wx * both_x + wy * both_y + vertical
        safe = jnp.where(covered, diagonal, 1.0)
        out.append(jnp.where(covered, 2.0 / safe, 0.0))
    return out


def sweep_kernel(
    layers,
    u_in, v_in, e_in, f_in, packed, packed_left, packed_right, basal_velocity,
    out, gradient, scale_out, eta_out, strip_out,
    fields, products, eta, scale, edges, sums,
):
    circle, cols = f_in.shape
    rows = out.shape[2]
    lane = lane_index((circle, cols))
    column = lane % GROUP
    omegas = omega_list(ITERS)
    zero = jnp.zeros((circle, cols), F32)

    strips = []
    for side in range(2):
        values = []
        for field in range(3):
            own = packed[field]
            if side == 0:
                values.append(jnp.where(column < HALO, packed_left[field], own))
            else:
                values.append(jnp.where(column < HALO, own, packed_right[field]))
        signed = values[2]
        inside = lane < GROUP * layers
        bottom = inside & (lane >= GROUP * (layers - 1))
        covered = inside & (signed > 0.0)
        e = jnp.where(inside, jnp.abs(signed), 0.0)
        basal = jnp.where(bottom, lanes_after(signed, GROUP), 0.0)
        ends = jnp.where(bottom | (lane < GROUP), 1.0, 2.0)
        pair = inverse_pair(
            e,
            rows_before(e) + rows_after(e),
            lanes_before(e) + lanes_after(e),
            lanes_before(e, GROUP) + lanes_after(e, GROUP),
            ends,
            basal,
            covered,
        )
        strip_out[side, 0] = e
        strip_out[side, 1] = pair[0]
        strip_out[side, 2] = pair[1]
        strips.append((e, pair, values[:2]))
    eta_edge = joined(strips[0][0], strips[1][0], column)
    states = [strips[0][2], strips[1][2]]
    for turn, omega in enumerate(omegas):
        step = omega if turn < ITERS - 1 else None
        left, lows, _ = strip_step(strips[0][0], strips[0][1], states[0], step)
        right, _, highs = strip_step(strips[1][0], strips[1][1], states[1], step)
        for c in range(2):
            edges[turn, c] = joined(states[0][c], states[1][c], column)
            sums[turn, c] = joined(lows[c], highs[c], column)
        states = [left, right]

    for stack in (eta, fields.at[0, 0], fields.at[0, 1], fields.at[1, 0], fields.at[1, 1]):
        stack[0] = zero
        stack[layers + 1] = zero
    for half in range(2):
        for c in range(2):
            products[half, c, 0] = zero
            products[half, c, layers + 1] = zero

    def load(k, carry):
        e = jnp.abs(e_in[k])
        eta[k + 1] = e
        for c, values in enumerate((u_in, v_in)):
            f = values[k]
            fields[0, c, k + 1] = f
            products[0, c, k + 1] = e * f
        return carry

    lax.fori_loop(0, layers, load, 0)

    def weigh(k, carry):
        e = eta[k + 1]
        edge = pltpu.roll(eta_edge, cols - (GROUP * k + HALO), 1)
        e_y = lanes_before(jnp.where(lane == cols - 1, edge, e))
        e_y = e_y + lanes_after(jnp.where(lane == 0, edge, e))
        is_end = (k == 0) | (k == layers - 1)
        ends = jnp.where(is_end, 1.0, 2.0)
        basal = jnp.where(k == layers - 1, 1.0, 0.0) * f_in[...]
        pair = inverse_pair(
            e,
            rows_before(e) + rows_after(e),
            e_y,
            eta[k] + eta[k + 2],
            ends,
            basal,
            e_in[k] > 0.0,
        )
        scale[0, k] = pair[0]
        scale[1, k] = pair[1]
        return carry

    lax.fori_loop(0, layers, weigh, 0)

    for turn, omega in enumerate(omegas):
        half, final = turn % 2, turn == ITERS - 1
        near = (edges.at[turn], sums.at[turn])

        def sweep(k, carry, half=half, final=final, near=near, omega=omega):
            pair = plane_step(
                k, lane, eta, fields.at[half], products.at[half], scale,
                (near[0][0], near[0][1]), (near[1][0], near[1][1]), omega,
            )
            for c in range(2):
                if final:
                    out[c, k] = pair[c][:rows]
                else:
                    fields[1 - half, c, k + 1] = pair[c]
                    products[1 - half, c, k + 1] = eta[k + 1] * pair[c]
            return carry

        lax.fori_loop(0, layers, sweep, 0)

    covered = e_in[layers - 1][:rows] > 0.0
    flow = basal_velocity[0] * out[0, layers - 1] + basal_velocity[1] * out[1, layers - 1]
    gradient[...] = jnp.where(covered, -f_in[...][:rows] * flow, 0.0)
    for k in range(ITERS):
        for c in range(2):
            scale_out[c, k] = scale[c, k]
    for k in range(ITERS + 1):
        eta_out[k] = eta[k + 1]


def free_sweeps(u, v, e, f, packed, left, right, basal_velocity):
    layers, circle, cols = u.shape
    rows = basal_velocity.shape[1]
    plane = (circle, cols)
    stack = (layers + 2,) + plane
    return pl.pallas_call(
        functools.partial(sweep_kernel, layers),
        in_specs=vmem_specs(8),
        out_specs=vmem_specs(5),
        out_shape=[
            jax.ShapeDtypeStruct((2, layers, rows, cols), F32),
            jax.ShapeDtypeStruct((rows, cols), F32),
            jax.ShapeDtypeStruct((2, ITERS) + plane, F32),
            jax.ShapeDtypeStruct((ITERS + 1,) + plane, F32),
            jax.ShapeDtypeStruct((2, 3) + plane, F32),
        ],
        scratch_shapes=[
            pltpu.VMEM((2, 2) + stack, F32),
            pltpu.VMEM((2, 2) + stack, F32),
            pltpu.VMEM(stack, F32),
            pltpu.VMEM((2, layers) + plane, F32),
            pltpu.VMEM((ITERS, 2) + plane, F32),
            pltpu.VMEM((ITERS, 2) + plane, F32),
        ],
        cost_estimate=pl.CostEstimate(
            flops=200_000_000, transcendentals=0, bytes_accessed=8_000_000
        ),
        compiler_params=pltpu.CompilerParams(vmem_limit_bytes=24 << 20),
        name="free_sweeps",
    )(u, v, e, f, packed, left, right, basal_velocity)


def pack_kernel(devices, capacity, units, tile, row, misfit, out, slot_vector, slot, sem):
    turns, lanes = tile.shape
    device = lax.broadcasted_iota(jnp.int32, (devices, lanes), 0)
    at_row = lax.broadcasted_iota(jnp.int32, (lanes, lanes), 0)
    at_lane = lax.broadcasted_iota(jnp.int32, (lanes, lanes), 1)
    earlier = jnp.where(at_row < at_lane, 1.0, 0.0).astype(BF16)
    seen = jnp.zeros((devices, 1), F32)
    keys = jnp.zeros((devices, lanes), F32)
    for turn in range(turns):
        target = tile[turn : turn + 1, :]
        onehot = jnp.where(device == target, 1.0, 0.0)
        before = jnp.dot(onehot.astype(BF16), earlier, preferred_element_type=F32) + seen
        rank = jnp.sum(onehot * before, axis=0, keepdims=True).astype(jnp.int32)
        slot_vector[turn : turn + 1, :] = target * units + rank
        seen = seen + jnp.sum(onehot, axis=1, keepdims=True)
        named = onehot * (row[turn : turn + 1, :] + 1).astype(F32)
        place = jnp.where(at_row // 2 == rank, 1.0, 0.0).astype(BF16)
        keys = keys + lax.dot_general(
            named.astype(BF16), place, (((1,), (1,)), ((), ())), preferred_element_type=F32
        )
    copy = pltpu.make_async_copy(slot_vector, slot, sem)
    copy.start()
    out[...] = jnp.zeros(out.shape, BF16)
    upper = lax.broadcasted_iota(jnp.int32, (2, lanes), 0) == 0
    for d in range(devices):
        both = jnp.where(upper, jnp.broadcast_to(keys[d : d + 1, :], (2, lanes)), 0.0)
        out[d * units + capacity] = both.astype(BF16)
    copy.wait()

    def place_row(turn, carry):
        for i in range(lanes):
            out[slot[turn, i]] = misfit[turn * lanes + i]
        return carry

    lax.fori_loop(0, turns, place_row, 0)


def pack_blocks(misfit, block_tile, block_row, devices):
    count, _, cols = misfit.shape
    capacity = 2 * count // devices
    units = capacity + PAD_UNITS
    grid_shape = (count // cols, cols)
    packed = pl.pallas_call(
        functools.partial(pack_kernel, devices, capacity, units),
        in_specs=vmem_specs(3),
        out_specs=pl.BlockSpec(memory_space=pltpu.VMEM),
        out_shape=jax.ShapeDtypeStruct((devices * units, 2, cols), BF16),
        scratch_shapes=[
            pltpu.VMEM(grid_shape, jnp.int32),
            pltpu.SMEM(grid_shape, jnp.int32),
            pltpu.SemaphoreType.DMA,
        ],
        compiler_params=pltpu.CompilerParams(vmem_limit_bytes=4 << 20),
        name="pack_blocks",
    )(block_tile.reshape(grid_shape), block_row.reshape(grid_shape), misfit)
    return packed.reshape(devices * units * 2, cols)


def surface_kernel(devices, capacity, units, got, surface, low, high):
    rows, lanes = surface.shape[1:]
    span = 2 * capacity
    group = max(1, lanes // span)
    at_row = lax.broadcasted_iota(jnp.int32, (2 * rows, lanes), 0).astype(F32)
    odd = (lax.broadcasted_iota(jnp.int32, (1, lanes), 1) % 2).astype(F32) * rows
    total = jnp.zeros((2 * rows, lanes), F32)
    for first in range(0, devices, group):
        key = None
        values = []
        for q in range(group):
            start = (first + q) * units * 2
            tile = got[start + span : start + span + 8, :].astype(F32)[:1, :]
            tile = pltpu.roll(tile, q * span, 1) if q else tile
            key = tile if key is None else key + tile
            values.append(got[start : start + span, :])
        wanted = jnp.where(key > 0.0, key - 1.0 + odd, -1.0)
        select = jnp.where(at_row == wanted, 1.0, 0.0).astype(BF16)
        block = values[0] if group == 1 else jnp.concatenate(values, axis=0)
        total = total + jnp.dot(select, block, preferred_element_type=F32)
    for c in range(2):
        surface[c] = total[c * rows : (c + 1) * rows]
    low[...] = jnp.zeros(low.shape, F32)
    high[...] = jnp.zeros(high.shape, F32)
    for c in range(2):
        low[2 * c : 2 * c + 2, :] = surface[c, :2, :]
        high[2 * c : 2 * c + 2, :] = surface[c, rows - 2 :, :]


def sum_blocks(got, devices, capacity, rows):
    cols = got.shape[1]
    edge = jax.ShapeDtypeStruct((8, cols), F32)
    return pl.pallas_call(
        functools.partial(surface_kernel, devices, capacity, capacity + PAD_UNITS),
        in_specs=vmem_specs(1),
        out_specs=vmem_specs(3),
        out_shape=[jax.ShapeDtypeStruct((2, rows, cols), F32), edge, edge],
        compiler_params=pltpu.CompilerParams(vmem_limit_bytes=4 << 20),
        name="sum_blocks",
    )(got)


def source_kernel(surface, above, below, source, packed):
    rows, cols = surface.shape[1:]
    circle = rows + 8
    for c in range(2):
        source[c, :rows, :] = surface[c]
        source[c, rows : rows + 2, :] = below[2 * c : 2 * c + 2, :]
        source[c, rows + 2 : circle - 2, :] = jnp.zeros((4, cols), F32)
        source[c, circle - 2 : circle, :] = above[2 * c : 2 * c + 2, :]
    lane = lane_index((circle, cols))
    first = jnp.where(lane < GROUP, lanes_before(source[0], HALO), 0.0)
    both = jnp.where(lane // GROUP == 1, lanes_before(source[1], HALO + GROUP), first)
    packed[...] = both


def source_columns(surface, above, below):
    _, rows, cols = surface.shape
    circle = rows + 8
    return pl.pallas_call(
        source_kernel,
        in_specs=vmem_specs(3),
        out_specs=vmem_specs(2),
        out_shape=[
            jax.ShapeDtypeStruct((2, circle, cols), F32),
            jax.ShapeDtypeStruct((circle, cols), F32),
        ],
        compiler_params=pltpu.CompilerParams(vmem_limit_bytes=2 << 20),
        name="source_columns",
    )(surface, above, below)


def response_kernel(
    source, packed, packed_left, packed_right, scale, eta_in, strip_in, adj_in,
    out, fields, products, eta,
):
    circle, cols = packed.shape
    rows = out.shape[2]
    lane = lane_index((circle, cols))
    column = lane % GROUP
    omegas = omega_list(ITERS)
    zero = jnp.zeros((circle, cols), F32)
    top = lane < GROUP

    strips = []
    for side in range(2):
        if side == 0:
            both = jnp.where(column < HALO, packed_left[...], packed[...])
        else:
            both = jnp.where(column < HALO, packed[...], packed_right[...])
        pair = (jnp.where(top, both, 0.0), jnp.where(top, lanes_after(both, GROUP), 0.0))
        strips.append((strip_in[side, 0], (strip_in[side, 1], strip_in[side, 2]), pair))
    states = [
        [(0.5 * omegas[0]) * (weight[c] * pair[c]) for c in range(2)] for _, weight, pair in strips
    ]
    near = []
    for turn in range(1, ITERS):
        omega = omegas[turn] if turn < ITERS - 1 else None
        left, lows, _ = strip_step(strips[0][0], strips[0][1], states[0], omega, strips[0][2])
        right, _, highs = strip_step(strips[1][0], strips[1][1], states[1], omega, strips[1][2])
        near.append(
            (
                [joined(states[0][c], states[1][c], column) for c in range(2)],
                [joined(lows[c], highs[c], column) for c in range(2)],
            )
        )
        states = [left, right]

    eta[0] = zero
    for k in range(ITERS + 1):
        eta[k + 1] = eta_in[k]
    for half in range(2):
        for c in range(2):
            for k in range(ITERS + 2):
                fields[half, c, k] = zero
                products[half, c, k] = zero
    drive = [0.5 * source[c] for c in range(2)]
    for c in range(2):
        f = omegas[0] * (scale[c, 0] * drive[c])
        fields[0, c, 1] = f
        products[0, c, 1] = eta[1] * f
    for turn in range(1, ITERS):
        half, final = (turn - 1) % 2, turn == ITERS - 1
        edges, sums = near[turn - 1]
        for k in range(turn + 1):
            pair = plane_step(
                k, lane, eta, fields.at[half], products.at[half], scale, edges, sums,
                omegas[turn], drive if k == 0 else None,
            )
            for c in range(2):
                if final:
                    out[c, k] = adj_in[c, k] + pair[c][:rows]
                else:
                    fields[1 - half, c, k + 1] = pair[c]
                    products[1 - half, c, k + 1] = eta[k + 1] * pair[c]


def add_response(source, packed, left, right, scale, eta, strips, adjoint):
    circle, cols = packed.shape
    _, _, rows, _ = adjoint.shape
    plane = (circle, cols)
    top = pl.BlockSpec((2, ITERS, rows, cols), lambda i: (0, 0, 0, 0))

    def whole(array):
        return pl.BlockSpec(array.shape, lambda i, n=array.ndim: (0,) * n)

    operands = (source, packed, left, right, scale, eta, strips)
    return pl.pallas_call(
        response_kernel,
        grid=(1,),
        in_specs=[whole(array) for array in operands] + [top],
        out_specs=top,
        out_shape=jax.ShapeDtypeStruct(adjoint.shape, F32),
        scratch_shapes=[
            pltpu.VMEM((2, 2, ITERS + 2) + plane, F32),
            pltpu.VMEM((2, 2, ITERS + 2) + plane, F32),
            pltpu.VMEM((ITERS + 2,) + plane, F32),
        ],
        input_output_aliases={7: 0},
        compiler_params=pltpu.CompilerParams(vmem_limit_bytes=8 << 20),
        name="add_response",
    )(*operands, adjoint)


def on_device(
    adjoint_prev, viscosity, friction, basal_velocity, ice_mask, misfit, block_tile, block_row
):
    devices = lax.axis_size("gx") * lax.axis_size("gy")
    layers, rows, cols = adjoint_prev.shape[1:]
    capacity = 2 * misfit.shape[0] // devices
    assert layers > 2 * ITERS and GROUP * (layers + 1) <= cols and rows % 8 == 0
    assert 2 * capacity <= cols and cols % (2 * capacity) == 0 and misfit.shape[0] % cols == 0

    edge_low, edge_high = edge_rows(adjoint_prev, viscosity, friction, ice_mask)
    above = shift_up(edge_high, "gx")
    below = shift_down(edge_low, "gx")
    sent = pack_blocks(misfit, block_tile, block_row, devices)
    got = lax.all_to_all(
        sent.reshape(devices, -1, cols), ("gx", "gy"), split_axis=0, concat_axis=0, tiled=True
    )
    u, v, e, f, packed = edge_columns(
        adjoint_prev, viscosity, friction, ice_mask, above, below
    )
    left = shift_up(packed, "gy")
    right = shift_down(packed, "gy")
    adjoint, gradient, scale, eta, strips = free_sweeps(
        u, v, e, f, packed, left, right, basal_velocity
    )
    surface, low, high = sum_blocks(got.reshape(-1, cols), devices, capacity, rows)
    source, source_packed = source_columns(
        surface, shift_up(high, "gx"), shift_down(low, "gx")
    )
    source_left = shift_up(source_packed, "gy")
    source_right = shift_down(source_packed, "gy")
    adjoint = add_response(
        source, source_packed, source_left, source_right, scale, eta, strips, adjoint
    )
    return (adjoint, gradient)


def solution(mesh):
    placed = (
        P(None, None, "gx", "gy"),
        P(None, "gx", "gy"),
        P("gx", "gy"),
        P(None, "gx", "gy"),
        P("gx", "gy"),
        P(("gx", "gy"), None, None),
        P(("gx", "gy"), None),
        P(("gx", "gy")),
    )

    return jax.shard_map(
        on_device,
        mesh=mesh,
        in_specs=placed,
        out_specs=(P(None, None, "gx", "gy"), P("gx", "gy")),
        check_vma=False,
    )
```

```python
import functools
import math

import jax
import jax.numpy as jnp
from jax import lax
from jax.experimental import pallas as pl
from jax.experimental.pallas import tpu as pltpu
from jax.sharding import PartitionSpec as P


ITERS = 3
HALO = ITERS
GROUP = 2 * HALO
VERTICAL = 4.0

F32 = jnp.float32
BF16 = jnp.bfloat16


def omega_list(count):
    return [
        1.0 / (1.3 + 1.2 * math.cos((2 * turn_id + 1) * math.pi / (2 * count)))
        for turn_id in range(count)
    ]


def shift_up(array, axis):
    peers = lax.axis_size(axis)
    return lax.ppermute(array, axis, [(i, i + 1) for i in range(peers - 1)])


def shift_down(array, axis):
    peers = lax.axis_size(axis)
    return lax.ppermute(array, axis, [(i + 1, i) for i in range(peers - 1)])


def vmem_specs(count):
    return [pl.BlockSpec(memory_space=pltpu.VMEM) for _ in range(count)]


LEAD = 8


def put_plane(ref, values):
    circle = values.shape[0]
    ref[LEAD : LEAD + circle, :] = values
    ref[LEAD - 1 : LEAD, :] = values[circle - 1 :, :]
    ref[LEAD + circle : LEAD + circle + 1, :] = values[:1, :]


def get_plane(ref, count, step=0):
    return ref[LEAD + step : LEAD + step + count, :]


def stored(circle):
    return circle + 2 * LEAD


def lanes_before(values, step=1):
    return pltpu.roll(values, step, 1)


def lanes_after(values, step=1):
    return pltpu.roll(values, values.shape[1] - step, 1)


def lane_index(shape):
    return lax.broadcasted_iota(jnp.int32, shape, len(shape) - 1)


def edge_kernel(layers, adj_lo, adj_hi, eta_lo, eta_hi, fr_lo, fr_hi, ice_lo, ice_hi, lo, hi):
    for adj, eta, fr, ice, out, at in (
        (adj_lo, eta_lo, fr_lo, ice_lo, lo, 0),
        (adj_hi, eta_hi, fr_hi, ice_hi, hi, 8 - HALO),
    ):
        rows = slice(at, at + HALO)
        covered = ice[rows, :] > 0
        for plane in range(2 * layers):
            values = jnp.where(covered, adj[plane // layers, plane % layers, rows, :], 0.0)
            out[HALO * plane : HALO * (plane + 1), :] = values
        for layer in range(layers):
            values = eta[layer, rows, :]
            first = HALO * (2 * layers + layer)
            out[first : first + HALO, :] = jnp.where(covered, values, -values)
        first = HALO * 3 * layers
        out[first : first + HALO, :] = fr[rows, :]


def edge_rows(adjoint, viscosity, friction, ice_mask):
    _, layers, rows, cols = adjoint.shape
    last = rows // 8 - 1
    length = -(-HALO * (3 * layers + 1) // 8) * 8

    def pair(block, index):
        return [
            pl.BlockSpec(block, functools.partial(index, 0)),
            pl.BlockSpec(block, functools.partial(index, last)),
        ]

    specs = pair((2, layers, 8, cols), lambda r, i: (0, 0, r, 0))
    specs += pair((layers, 8, cols), lambda r, i: (0, r, 0))
    specs += pair((8, cols), lambda r, i: (r, 0))
    specs += pair((8, cols), lambda r, i: (r, 0))
    return pl.pallas_call(
        functools.partial(edge_kernel, layers),
        grid=(1,),
        in_specs=specs,
        out_specs=[pl.BlockSpec((length, cols), lambda i: (0, 0))] * 2,
        out_shape=[jax.ShapeDtypeStruct((length, cols), F32)] * 2,
        compiler_params=pltpu.CompilerParams(vmem_limit_bytes=60 << 20),
        name="edge_rows",
    )(adjoint, adjoint, viscosity, viscosity, friction, friction, ice_mask, ice_mask)


def column_kernel(
    layers, adj, eta_in, fr, ice, above, below,
    fields, products, eta, cover, fr_out, packed, work,
):
    rows, cols = fr.shape
    circle = rows + 8
    lane_layer = lane_index((circle, cols)) // GROUP
    covered = ice[...] > 0
    gap = jnp.zeros((8 - 2 * HALO, cols), F32)
    zero = jnp.zeros((stored(circle), cols), F32)
    for end in (0, layers + 1):
        eta[end] = zero
        for c in range(2):
            fields[c, end] = zero
            products[c, end] = zero

    def extend(values, plane):
        first = HALO * plane
        slot = work.at[plane % 2]
        slot[:rows, :] = values
        slot[rows : rows + HALO, :] = below[first : first + HALO, :]
        slot[rows + HALO : circle - HALO, :] = gap
        slot[circle - HALO : circle, :] = above[first : first + HALO, :]
        return slot[...]

    def gather(total, values, layer):
        return jnp.where(
            lane_layer == layer, pltpu.roll(values, (HALO + GROUP * layer) % cols, 1), total
        )

    totals = [jnp.zeros((circle, cols), F32)] * 3
    for layer in range(layers):
        values = eta_in[layer]
        signed = extend(jnp.where(covered, values, -values), 2 * layers + layer)
        totals[2] = gather(totals[2], signed, layer)
        if layer == 0:
            cover[...] = jnp.where(signed > 0.0, 2.0, 0.0)
        e = jnp.abs(signed)
        put_plane(eta.at[layer + 1], e)
        for c in range(2):
            f = extend(jnp.where(covered, adj[c, layer], 0.0), c * layers + layer)
            totals[c] = gather(totals[c], f, layer)
            put_plane(fields.at[c, layer + 1], f)
            products[c, layer + 1, LEAD : LEAD + circle, :] = e * f
    values = extend(fr[...], 3 * layers)
    fr_out[...] = values
    totals[2] = gather(totals[2], values, layers)
    for field in range(3):
        packed[field] = totals[field]


def edge_columns(adjoint, viscosity, friction, ice_mask, above, below):
    _, layers, rows, cols = adjoint.shape
    circle = rows + 8
    stack = (layers + 2, stored(circle), cols)
    return pl.pallas_call(
        functools.partial(column_kernel, layers),
        in_specs=vmem_specs(6),
        out_specs=vmem_specs(6),
        out_shape=[
            jax.ShapeDtypeStruct((2,) + stack, F32),
            jax.ShapeDtypeStruct((2,) + stack, F32),
            jax.ShapeDtypeStruct(stack, F32),
            jax.ShapeDtypeStruct((circle, cols), F32),
            jax.ShapeDtypeStruct((circle, cols), F32),
            jax.ShapeDtypeStruct((3, circle, cols), F32),
        ],
        scratch_shapes=[pltpu.VMEM((2, circle, cols), F32)],
        compiler_params=pltpu.CompilerParams(vmem_limit_bytes=16 << 20),
        name="edge_columns",
    )(adjoint, viscosity, friction, ice_mask, above, below)


def keep_of(omega):
    return (1.0 - omega) / omega


def strip_step(eta, scale, fields, keep, work, sources=None):
    count = eta.shape[0]
    eta_half, eta_quarter = 0.5 * eta, 0.25 * eta
    parts = []
    for c, f in enumerate(fields):
        slot = work.at[c, 0]
        put_plane(slot, f)
        x_low, x_high = get_plane(slot, count, -1), get_plane(slot, count, 1)
        strong, weak = (eta_half, eta_quarter) if c == 0 else (eta_quarter, eta_half)
        part = dict(p=eta * f, h=weak * (x_high - x_low), sum_x=x_low + x_high)
        if keep is not None:
            y_low, y_high = lanes_before(f), lanes_after(f)
            p = part["p"]
            part["sum_y"] = y_low + y_high
            part["sum_z"] = lanes_before(f, GROUP) + lanes_after(f, GROUP)
            part["p_z"] = lanes_before(p, GROUP) + lanes_after(p, GROUP)
            part["g"] = strong * (y_high - y_low)
        parts.append(part)
    news, lows, highs = [], [], []
    for c in range(2):
        mine, other = parts[c], parts[1 - c]
        p = mine["p"]
        low, high = p - other["h"], p + other["h"]
        lows.append(low)
        highs.append(high)
        if keep is None:
            continue
        put_plane(work.at[c, 1], p + other["g"])
        put_plane(work.at[c, 2], p - other["g"])
        along_x = get_plane(work.at[c, 1], count, 1) + get_plane(work.at[c, 2], count, -1)
        along_y = lanes_after(high) + lanes_before(low)
        if c == 0:
            near = mine["sum_x"] + mine["sum_z"] + 0.25 * mine["sum_y"]
            rest = along_x + mine["p_z"] + 0.25 * along_y
        else:
            near = mine["sum_y"] + mine["sum_z"] + 0.25 * mine["sum_x"]
            rest = along_y + mine["p_z"] + 0.25 * along_x
        total = eta * near + rest
        if sources is not None:
            total = total + sources[c]
        news.append(keep * fields[c] + scale[c] * total)
    return news, lows, highs


def joined(left, right, column, at):
    return jnp.where(column == at, left, right)


def plane_step(k, count, lane, eta, fields, products, scale, keep, work, edges, source=None):
    circle, cols = lane.shape
    back = cols - (GROUP * k + HALO)
    first, last = lane == 0, lane == cols - 1
    e_all = get_plane(eta.at[k + 1], circle)
    eta_half, eta_quarter = 0.5 * e_all, 0.25 * e_all
    parts = []
    for c in range(2):
        slot = fields.at[c, k + 1]
        f = get_plane(slot, circle)
        low = high = f
        if edges is not None:
            edge = pltpu.roll(edges[0][c], back, 1)
            low, high = jnp.where(last, edge, f), jnp.where(first, edge, f)
        y_low, y_high = lanes_before(low), lanes_after(high)
        x_low, x_high = get_plane(slot, circle, -1), get_plane(slot, circle, 1)
        strong, weak = (eta_half, eta_quarter) if c == 0 else (eta_quarter, eta_half)
        parts.append(
            dict(
                f=f[:count],
                sum_x=(x_low + x_high)[:count],
                sum_y=(y_low + y_high)[:count],
                g=strong * (y_high - y_low),
                h=(weak * (x_high - x_low))[:count],
            )
        )
    e, first, last = e_all[:count], first[:count], last[:count]
    news = []
    for c in range(2):
        mine, other = parts[c], parts[1 - c]
        p = get_plane(products.at[c, k + 1], circle)
        put_plane(work.at[c, 0], p + other["g"])
        put_plane(work.at[c, 1], p - other["g"])
        along_x = get_plane(work.at[c, 0], count, 1) + get_plane(work.at[c, 1], count, -1)
        p = p[:count]
        low, high = p - other["h"], p + other["h"]
        if edges is not None:
            edge = pltpu.roll(edges[1][c][:count], back, 1)
            low, high = jnp.where(last, edge, low), jnp.where(first, edge, high)
        along_y = lanes_before(low) + lanes_after(high)
        sum_z = get_plane(fields.at[c, k], count) + get_plane(fields.at[c, k + 2], count)
        p_z = get_plane(products.at[c, k], count) + get_plane(products.at[c, k + 2], count)
        if c == 0:
            near = mine["sum_x"] + sum_z + 0.25 * mine["sum_y"]
            rest = along_x + p_z + 0.25 * along_y
        else:
            near = mine["sum_y"] + sum_z + 0.25 * mine["sum_x"]
            rest = along_y + p_z + 0.25 * along_x
        total = e * near + rest
        if source is not None:
            total = total + source[c][:count]
        news.append(keep * mine["f"] + scale[c, k][:count] * total)
    return news


def set_sides(k, lane, values, strips):
    cols = lane.shape[1]
    edge = pltpu.roll(strips, cols - (GROUP * k + HALO), 1)
    return jnp.where((lane == 0) | (lane == cols - 1), edge, values)


def inverse_pair(e, e_x, e_y, e_z, ends, basal, cover):
    double = 2.0 * e
    both_x, both_y = e_x + double, e_y + double
    vertical = (VERTICAL / 2) * (e_z + ends * e) + basal
    first = 2.0 * both_x + 0.5 * both_y + vertical
    second = 0.5 * both_x + 2.0 * both_y + vertical
    inverse = cover / jnp.where(cover > 0.0, first * second, 1.0)
    return inverse * second, inverse * first


def sweep_kernel(
    layers,
    fields_in, products_in, eta, cover, f_in, packed, packed_left, packed_right, basal_velocity,
    out, gradient, scale_out, eta_out, strip_out,
    fields, products, scale, strip_work, plane_work,
):
    circle, cols = f_in.shape
    rows = out.shape[2]
    lane = lane_index((circle, cols))
    column = lane % GROUP
    omegas = omega_list(ITERS)

    strips = []
    inside = lane < GROUP * layers
    bottom = inside & (lane >= GROUP * (layers - 1))
    ends = jnp.where(bottom | (lane < GROUP), 1.0, 2.0)
    for side in range(2):
        values = []
        for field in range(3):
            own = packed[field]
            if side == 0:
                values.append(jnp.where(column < HALO, packed_left[field], own))
            else:
                values.append(jnp.where(column < HALO, own, packed_right[field]))
        signed = values[2]
        e = jnp.where(inside, jnp.abs(signed), 0.0)
        basal = jnp.where(bottom, lanes_after(signed, GROUP), 0.0)
        slot = strip_work.at[side, 0, 0]
        put_plane(slot, e)
        pair = inverse_pair(
            e,
            get_plane(slot, circle, -1) + get_plane(slot, circle, 1),
            lanes_before(e) + lanes_after(e),
            lanes_before(e, GROUP) + lanes_after(e, GROUP),
            ends,
            basal,
            jnp.where(inside & (signed > 0.0), 2.0, 0.0),
        )
        strip_out[side, 0] = e
        strip_out[side, 1] = pair[0]
        strip_out[side, 2] = pair[1]
        strips.append((e, pair, values[:2]))
    eta_edge = joined(strips[0][0], strips[1][0], column, HALO - 1)

    def weigh(k, carry):
        slot = eta.at[k + 1]
        e = get_plane(slot, circle)
        edge = pltpu.roll(eta_edge, cols - (GROUP * k + HALO), 1)
        e_y = lanes_before(jnp.where(lane == cols - 1, edge, e))
        e_y = e_y + lanes_after(jnp.where(lane == 0, edge, e))
        is_end = (k == 0) | (k == layers - 1)
        pair = inverse_pair(
            e,
            get_plane(slot, circle, -1) + get_plane(slot, circle, 1),
            e_y,
            get_plane(eta.at[k], circle) + get_plane(eta.at[k + 2], circle),
            jnp.where(is_end, 1.0, 2.0),
            jnp.where(k == layers - 1, 1.0, 0.0) * f_in[...],
            cover[...],
        )
        scale[0, k] = pair[0]
        scale[1, k] = pair[1]
        return carry

    lax.fori_loop(0, layers, weigh, 0)

    zero = jnp.zeros((stored(circle), cols), F32)
    for half in range(ITERS - 1):
        for end in (0, layers + 1):
            for c in range(2):
                fields[half, c, end] = zero
                products[half, c, end] = zero

    states = [strips[0][2], strips[1][2]]
    source_fields, source_products = fields_in, products_in
    for turn, omega in enumerate(omegas):
        final = turn == ITERS - 1
        keep = None if final else keep_of(omega)
        left, lows, _ = strip_step(strips[0][0], strips[0][1], states[0], keep, strip_work.at[0])
        right, _, highs = strip_step(strips[1][0], strips[1][1], states[1], keep, strip_work.at[1])
        edges = sides = None
        if final:
            edges = tuple(
                [joined(low[c], high[c], column, HALO - 1) for c in range(2)]
                for low, high in ((states[0], states[1]), (lows, highs))
            )
        else:
            sides = [joined(left[c], right[c], column, HALO) for c in range(2)]
        states = [left, right]
        total = math.prod(omegas)

        def sweep(
            k, slot, final=final, keep=keep_of(omega), edges=edges, sides=sides,
            old=(source_fields, source_products), turn=turn,
        ):
            count = rows if final else circle
            pair = plane_step(
                k, count, lane, eta, old[0], old[1], scale, keep, plane_work.at[slot], edges
            )
            for c in range(2):
                if final:
                    out[c, k] = total * pair[c]
                else:
                    values = set_sides(k, lane, pair[c], sides[c])
                    put_plane(fields.at[turn, c, k + 1], values)
                    products[turn, c, k + 1, LEAD : LEAD + circle, :] = (
                        get_plane(eta.at[k + 1], circle) * values
                    )

        def pair_of(i, carry, sweep=sweep):
            for slot in range(UNROLL):
                sweep(UNROLL * i + slot, slot)
            return carry

        lax.fori_loop(0, layers // UNROLL, pair_of, 0)
        for k in range(layers // UNROLL * UNROLL, layers):
            sweep(k, k % UNROLL)
        if not final:
            source_fields, source_products = fields.at[turn], products.at[turn]

    covered = cover[...][:rows] > 0.0
    flow = basal_velocity[0] * out[0, layers - 1] + basal_velocity[1] * out[1, layers - 1]
    gradient[...] = jnp.where(covered, -f_in[...][:rows] * flow, 0.0)
    for k in range(ITERS):
        for c in range(2):
            scale_out[c, k] = scale[c, k]
    for k in range(ITERS + 1):
        eta_out[k] = eta[k + 1]


UNROLL = 2


def free_sweeps(fields, products, eta, cover, f, packed, left, right, basal_velocity):
    layers = eta.shape[0] - 2
    circle, cols = f.shape
    rows = basal_velocity.shape[1]
    plane = (circle, cols)
    kept = (stored(circle), cols)
    stack = (layers + 2,) + kept
    return pl.pallas_call(
        functools.partial(sweep_kernel, layers),
        in_specs=vmem_specs(9),
        out_specs=vmem_specs(5),
        out_shape=[
            jax.ShapeDtypeStruct((2, layers, rows, cols), F32),
            jax.ShapeDtypeStruct((rows, cols), F32),
            jax.ShapeDtypeStruct((2, ITERS) + plane, F32),
            jax.ShapeDtypeStruct((ITERS + 1,) + kept, F32),
            jax.ShapeDtypeStruct((2, 3) + plane, F32),
        ],
        scratch_shapes=[
            pltpu.VMEM((ITERS - 1, 2) + stack, F32),
            pltpu.VMEM((ITERS - 1, 2) + stack, F32),
            pltpu.VMEM((2, layers) + plane, F32),
            pltpu.VMEM((2, 2, 3) + kept, F32),
            pltpu.VMEM((UNROLL, 2, 2) + kept, F32),
        ],
        compiler_params=pltpu.CompilerParams(vmem_limit_bytes=24 << 20),
        cost_estimate=pl.CostEstimate(
            flops=200_000_000, transcendentals=0, bytes_accessed=8_000_000
        ),
        name="free_sweeps",
    )(fields, products, eta, cover, f, packed, left, right, basal_velocity)


EXTRA = 12
CORNER = 16


def pack_kernel(capacity, tile_in, row_in, misfit_in, out, keys_out, counts_out,
                tile, row, misfit, slot_vector, slot, sems):
    copies = [
        pltpu.make_async_copy(source, target, sems.at[i])
        for i, (source, target) in enumerate(
            ((tile_in, tile), (row_in, row), (misfit_in, misfit))
        )
    ]
    for copy in copies:
        copy.start()
    turns, lanes = tile.shape
    devices = keys_out.shape[0]
    device = lax.broadcasted_iota(jnp.int32, (devices, lanes), 0)
    at_row = lax.broadcasted_iota(jnp.int32, (lanes, lanes), 0)
    at_lane = lax.broadcasted_iota(jnp.int32, (lanes, lanes), 1)
    earlier = jnp.where(at_row < at_lane, 1.0, 0.0).astype(BF16)
    copies[0].wait()
    seen = jnp.zeros((devices, 1), F32)
    onehots, ranks = [], []
    for turn in range(turns):
        target = tile[turn : turn + 1, :]
        onehot = jnp.where(device == target, 1.0, 0.0)
        before = jnp.dot(onehot.astype(BF16), earlier, preferred_element_type=F32) + seen
        rank = jnp.sum(onehot * before, axis=0, keepdims=True).astype(jnp.int32)
        slot_vector[turn : turn + 1, :] = target * capacity + rank
        seen = seen + jnp.sum(onehot, axis=1, keepdims=True)
        onehots.append(onehot)
        ranks.append(rank)
    copy = pltpu.make_async_copy(slot_vector, slot, sems.at[3])
    copy.start()
    counts_out[...] = jnp.broadcast_to(seen, counts_out.shape)
    copies[1].wait()
    keys = jnp.zeros((devices, lanes), F32)
    for turn in range(turns):
        named = onehots[turn] * (row[turn : turn + 1, :] + 1).astype(F32)
        place = jnp.where(at_row // 2 == ranks[turn], 1.0, 0.0).astype(BF16)
        keys = keys + lax.dot_general(
            named.astype(BF16), place, (((1,), (1,)), ((), ())), preferred_element_type=F32
        )
    keys_out[...] = keys
    copies[2].wait()
    copy.wait()

    def place_row(turn, carry):
        for i in range(lanes):
            out[slot[turn, i]] = misfit[turn * lanes + i]
        return carry

    lax.fori_loop(0, turns, place_row, 0)


def pack_blocks(misfit, block_tile, block_row, devices, capacity):
    count, _, cols = misfit.shape
    grid_shape = (count // cols, cols)
    return pl.pallas_call(
        functools.partial(pack_kernel, capacity),
        in_specs=[pl.BlockSpec(memory_space=pltpu.HBM)] * 3,
        out_specs=vmem_specs(3),
        out_shape=[
            jax.ShapeDtypeStruct((devices * capacity, 2, cols), BF16),
            jax.ShapeDtypeStruct((devices, cols), F32),
            jax.ShapeDtypeStruct((devices, cols), F32),
        ],
        scratch_shapes=[
            pltpu.VMEM(grid_shape, jnp.int32),
            pltpu.VMEM(grid_shape, jnp.int32),
            pltpu.VMEM(misfit.shape, BF16),
            pltpu.VMEM(grid_shape, jnp.int32),
            pltpu.SMEM(grid_shape, jnp.int32),
            pltpu.SemaphoreType.DMA((4,)),
        ],
        compiler_params=pltpu.CompilerParams(vmem_limit_bytes=4 << 20),
        name="pack_blocks",
    )(block_tile.reshape(grid_shape), block_row.reshape(grid_shape), misfit)


def wanted_of(keys, rows):
    odd = lax.broadcasted_iota(jnp.int32, keys.shape, 1) % 2
    return jnp.where(keys > 0.0, keys - 1.0 + odd.astype(F32) * rows, -1.0)


def halves(values):
    high = values.astype(BF16).astype(F32)
    return jnp.concatenate([high, values - high], axis=0)


def bundle_kernel(devices, across, capacity, rows, slots, keys, counts, out, upper, lower, column):
    lanes = slots.shape[1]
    span = 2 * capacity
    place = span + 2 * EXTRA
    at_row = lax.broadcasted_iota(jnp.int32, (span, lanes), 0).astype(F32)
    line = lax.broadcasted_iota(jnp.int32, (8, lanes), 0)
    lane = lax.broadcasted_iota(jnp.int32, (8, lanes), 1)
    ends = jnp.where(line < 4, rows - 2, 0) + (line // 2 % 2) * rows + line % 2
    ends = ends[:, :span].astype(F32)
    pick = (line == 1) & (lane == lanes - 2) | (line == 2) & (lane == lanes - 1)
    pick = pick | (line == 3) & (lane == 0) | (line == 4) & (lane == 1)
    pick = jnp.where(pick, 1.0, 0.0).astype(BF16)
    for t in range(devices):
        used = 2.0 * counts[t : t + 1, :]
        block = slots[span * t : span * (t + 1), :].astype(F32)
        block = jnp.where(at_row < used, block, 0.0).astype(BF16)
        out[place * t : place * t + span, :] = block
        wanted = wanted_of(keys[t : t + 1, :], rows)[:, :span]
        select = jnp.where(ends == wanted, 1.0, 0.0).astype(BF16)
        found = jnp.dot(select, block, preferred_element_type=F32)
        upper[t] = halves(found[:4])
        lower[t] = halves(found[4:])
        side = lax.dot_general(
            pick, block, (((1,), (1,)), ((), ())), preferred_element_type=F32
        )
        if span < lanes:
            side = jnp.concatenate([side, jnp.zeros((8, lanes - span), F32)], axis=1)
        column[t] = side
    zero_row = jnp.zeros((1, lanes), F32)
    zero_edge = jnp.zeros((8, lanes), F32)
    for t in range(devices):
        has_left, has_right = t % across > 0, t % across < across - 1
        has_above, has_below = t >= across, t < devices - across
        above = upper[t - across] if has_above else zero_edge
        below = lower[t + across] if has_below else zero_edge
        corner = zero_edge
        for near, there, edge, first in (
            (t - across, has_above, upper, 0),
            (t + across, has_below, lower, 8),
        ):
            if there and has_left:
                value = pltpu.roll(edge[near - 1], HALO + first, 1)
                corner = jnp.where((lane == first + 1) | (lane == first + 2), value, corner)
            if there and has_right:
                value = pltpu.roll(edge[near + 1], HALO + first, 1)
                corner = jnp.where((lane == first + 3) | (lane == first + 4), value, corner)
        corner = pltpu.roll(corner, 0, 1, stride=CORNER, stride_axis=0)
        corner = jnp.sum(corner, axis=0, keepdims=True)
        key_left = keys[t - 1 : t, :] if has_left else zero_row
        key_right = keys[t + 1 : t + 2, :] if has_right else zero_row
        left = column[t - 1, 1:3, :] if has_left else zero_edge[:2]
        right = column[t + 1, 3:5, :] if has_right else zero_edge[:2]
        head = jnp.concatenate(
            [keys[t : t + 1, :], key_left, key_right, corner, left, right], axis=0
        )
        extra = jnp.concatenate([head, above, below], axis=0).astype(BF16)
        out[place * t + span : place * (t + 1), :] = extra


def bundle_blocks(slots, keys, counts, across, capacity, rows):
    devices, cols = keys.shape
    length = devices * 2 * (capacity + EXTRA)
    edge = pltpu.VMEM((devices, 8, cols), F32)
    return pl.pallas_call(
        functools.partial(bundle_kernel, devices, across, capacity, rows),
        in_specs=vmem_specs(3),
        out_specs=pl.BlockSpec(memory_space=pltpu.VMEM),
        out_shape=jax.ShapeDtypeStruct((length, cols), BF16),
        scratch_shapes=[edge, edge, edge],
        compiler_params=pltpu.CompilerParams(vmem_limit_bytes=8 << 20),
        name="bundle_blocks",
    )(slots, keys, counts)


def source_of(devices, capacity, rows, got, source, beside):
    lanes = got.shape[1]
    circle = rows + 8
    span = 2 * capacity
    place = span + 2 * EXTRA
    group = max(1, lanes // span)
    at_row = lax.broadcasted_iota(jnp.int32, (2 * rows, lanes), 0).astype(F32)
    line = lax.broadcasted_iota(jnp.int32, (8, lanes), 0)
    total = jnp.zeros((2 * rows, lanes), F32)
    side = jnp.zeros((2 * rows, 8), F32)
    extra_sum = jnp.zeros((2 * EXTRA, lanes), F32)
    contract = (((1,), (1,)), ((), ()))
    for first in range(0, devices, group):
        keys, blocks = None, []
        for q in range(group):
            start = (first + q) * place
            extra = got[start + span : start + place, :].astype(F32)
            extra_sum = extra_sum + extra
            head = pltpu.roll(extra[:8], q * span, 1) if q else extra[:8]
            keys = head if keys is None else keys + head
            blocks.append(got[start : start + span, :])
        wanted = wanted_of(keys[:3], rows)
        block = blocks[0] if group == 1 else jnp.concatenate(blocks, axis=0)
        picks = [
            jnp.where(at_row == wanted[i : i + 1], 1.0, 0.0).astype(BF16) for i in range(3)
        ]
        total = total + jnp.dot(picks[0], block, preferred_element_type=F32)
        low = jnp.where((line == 1) | (line == 2), pltpu.roll(keys, 5, 0), 0.0).astype(BF16)
        high = jnp.where((line == 3) | (line == 4), pltpu.roll(keys, 5, 0), 0.0).astype(BF16)
        side = side + lax.dot_general(picks[1], low, contract, preferred_element_type=F32)
        side = side + lax.dot_general(picks[2], high, contract, preferred_element_type=F32)
    above = extra_sum[8:12] + extra_sum[12:16]
    below = extra_sum[16:20] + extra_sum[20:24]
    lane = lax.broadcasted_iota(jnp.int32, (8, lanes), 1)
    corner = jnp.where(lane // CORNER == 7 - line, extra_sum[3:4], 0.0)
    corner = pltpu.roll(corner, lanes - 7 * CORNER, 1, stride=CORNER, stride_axis=0)
    corner = corner[:4] + corner[4:]
    corner = jnp.concatenate([corner[3 - i : 4 - i] for i in range(4)], axis=0)
    corner_below = pltpu.roll(corner, lanes - 8, 1)
    side = jnp.concatenate([side, jnp.zeros((2 * rows, lanes - 8), F32)], axis=1)
    gap = jnp.zeros((4, lanes), F32)
    for c in range(2):
        for target, inner, after, before in (
            (source, total, below, above),
            (beside, side, corner_below, corner),
        ):
            target[c, :rows, :] = inner[c * rows : (c + 1) * rows]
            target[c, rows : rows + 2, :] = after[2 * c : 2 * c + 2]
            target[c, rows + 2 : circle - 2, :] = gap
            target[c, circle - 2 : circle, :] = before[2 * c : 2 * c + 2]


def response_kernel(
    devices, capacity,
    got, scale, eta_in, strip_in, adj_in,
    out, source, beside, fields, products, eta, strip_work, plane_work,
):
    circle, cols = source.shape[1:]
    rows = out.shape[2]
    source_of(devices, capacity, rows, got, source, beside)
    lane = lane_index((circle, cols))
    column = lane % GROUP
    omegas = omega_list(ITERS)
    zero = jnp.zeros((stored(circle), cols), F32)
    top = lane < GROUP

    owns = [lanes_before(source[c], HALO) for c in range(2)]
    states, drives, weights = [], [], []
    for side in range(2):
        drive = []
        for c in range(2):
            if side == 0:
                both = jnp.where(column < HALO, beside[c], owns[c])
            else:
                both = jnp.where(column < HALO, owns[c], beside[c])
            drive.append(jnp.where(top, 0.5 * both, 0.0))
        weight = (strip_in[side, 1], strip_in[side, 2])
        states.append([weight[c] * drive[c] for c in range(2)])
        drives.append(drive)
        weights.append(weight)

    eta[0] = zero
    for k in range(ITERS + 1):
        eta[k + 1] = eta_in[k]
    for half in range(2):
        for c in range(2):
            for k in range(ITERS + 2):
                fields[half, c, k] = zero
                products[half, c, k] = zero
    drive = [0.5 * source[c] for c in range(2)]
    for c in range(2):
        f = scale[c, 0] * drive[c]
        put_plane(fields.at[0, c, 1], f)
        products[0, c, 1, LEAD : LEAD + circle, :] = get_plane(eta.at[1], circle) * f
    reach = omegas[0]
    for turn in range(1, ITERS):
        final = turn == ITERS - 1
        keep = None if final else keep_of(omegas[turn])
        part = 1.0 / reach
        new, lows, highs = [], None, None
        for side in range(2):
            values, low, high = strip_step(
                strip_in[side, 0], weights[side], states[side], keep, strip_work.at[side],
                [part * drives[side][c] for c in range(2)],
            )
            new.append(values)
            if side == 0:
                lows = low
            else:
                highs = high
        edges = sides = None
        if final:
            edges = tuple(
                [joined(low[c], high[c], column, HALO - 1) for c in range(2)]
                for low, high in ((states[0], states[1]), (lows, highs))
            )
        else:
            sides = [joined(new[0][c], new[1][c], column, HALO) for c in range(2)]
        states = new
        half = turn - 1
        scaled = [part * drive[c] for c in range(2)]
        for k in range(turn + 1):
            pair = plane_step(
                k, rows if final else circle, lane, eta, fields.at[half], products.at[half],
                scale, keep_of(omegas[turn]), plane_work.at[k % 2], edges,
                scaled if k == 0 else None,
            )
            for c in range(2):
                if final:
                    out[c, k] = adj_in[c, k] + (reach * omegas[turn]) * pair[c]
                else:
                    values = set_sides(k, lane, pair[c], sides[c])
                    put_plane(fields.at[turn, c, k + 1], values)
                    products[turn, c, k + 1, LEAD : LEAD + circle, :] = (
                        get_plane(eta.at[k + 1], circle) * values
                    )
        reach = reach * omegas[turn]


def add_response(got, devices, capacity, scale, eta, strips, adjoint):
    circle, cols = scale.shape[2:]
    _, _, rows, _ = adjoint.shape
    plane = (circle, cols)
    kept = (stored(circle), cols)
    top = pl.BlockSpec((2, ITERS, rows, cols), lambda i: (0, 0, 0, 0))

    def whole(array):
        return pl.BlockSpec(array.shape, lambda i, n=array.ndim: (0,) * n)

    operands = (got, scale, eta, strips)
    return pl.pallas_call(
        functools.partial(response_kernel, devices, capacity),
        grid=(1,),
        in_specs=[whole(array) for array in operands] + [top],
        out_specs=top,
        out_shape=jax.ShapeDtypeStruct(adjoint.shape, F32),
        scratch_shapes=[
            pltpu.VMEM((2,) + plane, F32),
            pltpu.VMEM((2,) + plane, F32),
            pltpu.VMEM((2, 2, ITERS + 2) + kept, F32),
            pltpu.VMEM((2, 2, ITERS + 2) + kept, F32),
            pltpu.VMEM((ITERS + 2,) + kept, F32),
            pltpu.VMEM((2, 2, 3) + kept, F32),
            pltpu.VMEM((2, 2, 2) + kept, F32),
        ],
        input_output_aliases={4: 0},
        compiler_params=pltpu.CompilerParams(vmem_limit_bytes=12 << 20),
        name="add_response",
    )(*operands, adjoint)


def on_device(
    adjoint_prev, viscosity, friction, basal_velocity, ice_mask, misfit, block_tile, block_row
):
    devices = lax.axis_size("gx") * lax.axis_size("gy")
    layers, rows, cols = adjoint_prev.shape[1:]
    capacity = 2 * misfit.shape[0] // devices
    assert layers > 2 * ITERS and GROUP * (layers + 1) <= cols and rows % 8 == 0
    assert 2 * capacity <= cols and cols % (2 * capacity) == 0 and misfit.shape[0] % cols == 0

    edge_low, edge_high = edge_rows(adjoint_prev, viscosity, friction, ice_mask)
    above = shift_up(edge_high, "gx")
    below = shift_down(edge_low, "gx")
    slots, keys, counts = pack_blocks(misfit, block_tile, block_row, devices, capacity)
    sent = bundle_blocks(
        slots.reshape(-1, cols), keys, counts, lax.axis_size("gy"), capacity, rows
    )
    got = lax.all_to_all(
        sent.reshape(devices, -1, cols), ("gx", "gy"), split_axis=0, concat_axis=0, tiled=True
    )
    stacks = edge_columns(adjoint_prev, viscosity, friction, ice_mask, above, below)
    packed = stacks[-1]
    left = shift_up(packed, "gy")
    right = shift_down(packed, "gy")
    adjoint, gradient, scale, eta, strips = free_sweeps(*stacks, left, right, basal_velocity)
    adjoint = add_response(
        got.reshape(-1, cols), devices, capacity, scale, eta, strips, adjoint
    )
    return (adjoint, gradient)


def solution(mesh):
    placed = (
        P(None, None, "gx", "gy"),
        P(None, "gx", "gy"),
        P("gx", "gy"),
        P(None, "gx", "gy"),
        P("gx", "gy"),
        P(("gx", "gy"), None, None),
        P(("gx", "gy"), None),
        P(("gx", "gy")),
    )

    return jax.shard_map(
        on_device,
        mesh=mesh,
        in_specs=placed,
        out_specs=(P(None, None, "gx", "gy"), P("gx", "gy")),
        check_vma=False,
    )
```

```python
import functools
import math

import jax
import jax.numpy as jnp
from jax import lax
from jax.experimental import pallas as pl
from jax.experimental.pallas import tpu as pltpu
from jax.sharding import PartitionSpec as P


ITERS = 3
HALO = ITERS
GROUP = 2 * HALO
VERTICAL = 4.0

F32 = jnp.float32
BF16 = jnp.bfloat16


def omega_list(count):
    return [
        1.0 / (1.3 + 1.2 * math.cos((2 * turn_id + 1) * math.pi / (2 * count)))
        for turn_id in range(count)
    ]


def shift_up(array, axis):
    peers = lax.axis_size(axis)
    return lax.ppermute(array, axis, [(i, i + 1) for i in range(peers - 1)])


def shift_down(array, axis):
    peers = lax.axis_size(axis)
    return lax.ppermute(array, axis, [(i + 1, i) for i in range(peers - 1)])


def vmem_specs(count):
    return [pl.BlockSpec(memory_space=pltpu.VMEM) for _ in range(count)]


LEAD = 8


def stored(circle):
    return circle + 2 * LEAD


def tile_of(ref, r, step=0):
    return ref[LEAD + 8 * r + step : LEAD + 8 * (r + 1) + step, :]


def put_tile(ref, r, values, tiles):
    ref[LEAD + 8 * r : LEAD + 8 * (r + 1), :] = values
    if r == tiles - 1:
        ref[LEAD - 1 : LEAD, :] = values[7:, :]
    if r == 0:
        ref[LEAD + 8 * tiles : LEAD + 8 * tiles + 1, :] = values[:1, :]


def rows_of(r):
    return slice(8 * r, 8 * (r + 1))


def lanes_before(values, step=1):
    return pltpu.roll(values, step, 1)


def lanes_after(values, step=1):
    return pltpu.roll(values, values.shape[1] - step, 1)


def lane_index(shape):
    return lax.broadcasted_iota(jnp.int32, shape, len(shape) - 1)


def extend(slot, values, above, below, plane):
    rows = values.shape[0]
    circle = slot.shape[0]
    first = HALO * plane
    slot[:rows, :] = values
    slot[rows : rows + HALO, :] = below[first : first + HALO, :]
    slot[rows + HALO : circle - HALO, :] = jnp.zeros((8 - 2 * HALO, values.shape[1]), F32)
    slot[circle - HALO : circle, :] = above[first : first + HALO, :]
    return slot


def in_turn(tiles, front, back, count=None):
    done = {tiles - 1: front(tiles - 1), 0: front(0)}
    count = tiles if count is None else count
    for r in range(1, tiles - 1):
        done[r] = front(r)
        back(r - 1, done[r - 1])
    for r in range(tiles - 2, count):
        back(r, done[r])


def edge_kernel(layers, adj_lo, adj_hi, eta_lo, eta_hi, fr_lo, fr_hi, ice_lo, ice_hi, lo, hi):
    for adj, eta, fr, ice, out, at in (
        (adj_lo, eta_lo, fr_lo, ice_lo, lo, 0),
        (adj_hi, eta_hi, fr_hi, ice_hi, hi, 8 - HALO),
    ):
        rows = slice(at, at + HALO)
        covered = ice[rows, :] > 0
        for plane in range(2 * layers):
            values = jnp.where(covered, adj[plane // layers, plane % layers, rows, :], 0.0)
            out[HALO * plane : HALO * (plane + 1), :] = values
        for layer in range(layers):
            values = eta[layer, rows, :]
            first = HALO * (2 * layers + layer)
            out[first : first + HALO, :] = jnp.where(covered, values, -values)
        first = HALO * 3 * layers
        out[first : first + HALO, :] = fr[rows, :]


def edge_rows(adjoint, viscosity, friction, ice_mask):
    _, layers, rows, cols = adjoint.shape
    last = rows // 8 - 1
    length = -(-HALO * (3 * layers + 1) // 8) * 8

    def pair(block, index):
        return [
            pl.BlockSpec(block, functools.partial(index, 0)),
            pl.BlockSpec(block, functools.partial(index, last)),
        ]

    specs = pair((2, layers, 8, cols), lambda r, i: (0, 0, r, 0))
    specs += pair((layers, 8, cols), lambda r, i: (0, r, 0))
    specs += pair((8, cols), lambda r, i: (r, 0))
    specs += pair((8, cols), lambda r, i: (r, 0))
    return pl.pallas_call(
        functools.partial(edge_kernel, layers),
        grid=(1,),
        in_specs=specs,
        out_specs=[pl.BlockSpec((length, cols), lambda i: (0, 0))] * 2,
        out_shape=[jax.ShapeDtypeStruct((length, cols), F32)] * 2,
        compiler_params=pltpu.CompilerParams(vmem_limit_bytes=60 << 20),
        name="edge_rows",
    )(adjoint, adjoint, viscosity, viscosity, friction, friction, ice_mask, ice_mask)


def column_kernel(layers, adj, eta, fr, ice, above, below, packed, work):
    rows, cols = fr.shape
    circle = rows + 8
    lane_layer = lane_index((circle, cols)) // GROUP
    covered = ice[...] > 0

    def gather(total, values, layer):
        return jnp.where(
            lane_layer == layer, pltpu.roll(values, (HALO + GROUP * layer) % cols, 1), total
        )

    for field in range(3):
        total = jnp.zeros((circle, cols), F32)
        for layer in range(layers):
            if field == 2:
                values = jnp.where(covered, eta[layer], -eta[layer])
            else:
                values = jnp.where(covered, adj[field, layer], 0.0)
            slot = extend(work.at[layer % 2], values, above, below, field * layers + layer)
            total = gather(total, slot[...], layer)
        if field == 2:
            slot = extend(work.at[layers % 2], fr[...], above, below, 3 * layers)
            total = gather(total, slot[...], layers)
        packed[field] = total


def edge_columns(adjoint, viscosity, friction, ice_mask, above, below):
    _, layers, rows, cols = adjoint.shape
    circle = rows + 8
    return pl.pallas_call(
        functools.partial(column_kernel, layers),
        in_specs=vmem_specs(6),
        out_specs=pl.BlockSpec(memory_space=pltpu.VMEM),
        out_shape=jax.ShapeDtypeStruct((3, circle, cols), F32),
        scratch_shapes=[pltpu.VMEM((2, circle, cols), F32)],
        compiler_params=pltpu.CompilerParams(vmem_limit_bytes=4 << 20),
        name="edge_columns",
    )(adjoint, viscosity, friction, ice_mask, above, below)


def keep_of(omega):
    return (1.0 - omega) / omega


def cross_factors(c, e):
    half, quarter = 0.5 * e, 0.25 * e
    return (half, quarter) if c == 0 else (quarter, half)


def gathered(c, e, sum_x, sum_y, along_x, along_y):
    strong, weak = (0, 1) if c == 0 else (1, 0)
    sums, alongs = (sum_x, sum_y), (along_x, along_y)
    return e * (sums[strong] + 0.25 * sums[weak]) + (alongs[strong] + 0.25 * alongs[weak])


def strip_planes(strip, signed, layers, scratch):
    circle, cols = signed.shape
    tiles = circle // 8
    lane = lane_index((8, cols))
    inside = lane < GROUP * layers
    bottom = inside & (lane >= GROUP * (layers - 1))
    ends = jnp.where(bottom | (lane < GROUP), 1.0, 2.0)
    for r in range(tiles):
        e = jnp.where(inside, jnp.abs(signed[rows_of(r)]), 0.0)
        put_tile(scratch, r, e, tiles)
        strip[0, rows_of(r), :] = e
    for r in range(tiles):
        e = tile_of(scratch, r)
        here = signed[rows_of(r)]
        z_low, z_high = lanes_before(e, GROUP), lanes_after(e, GROUP)
        strip[3, rows_of(r), :] = e + z_low
        strip[4, rows_of(r), :] = e + z_high
        pair = inverse_pair(
            e,
            tile_of(scratch, r, -1) + tile_of(scratch, r, 1),
            lanes_before(e) + lanes_after(e),
            z_low + z_high,
            ends,
            jnp.where(bottom, lanes_after(here, GROUP), 0.0),
            jnp.where(inside & (here > 0.0), 2.0, 0.0),
        )
        strip[1, rows_of(r), :], strip[2, rows_of(r), :] = pair


def strip_sweep(strip, fields, news, keep, work, source=None):
    tiles = strip.shape[1] // 8

    def front(r):
        e = strip[0, rows_of(r), :]
        parts = []
        for c in range(2):
            f = tile_of(fields.at[c], r)
            y_low, y_high = lanes_before(f), lanes_after(f)
            x_low, x_high = tile_of(fields.at[c], r, -1), tile_of(fields.at[c], r, 1)
            wg, wh = cross_factors(c, e)
            part = dict(f=f, p=e * f, g=wg * (y_high - y_low), h=wh * (x_high - x_low))
            part.update(sum_x=x_low + x_high, sum_y=y_low + y_high)
            parts.append(part)
        for c in range(2):
            p, g = parts[c]["p"], parts[1 - c]["g"]
            put_tile(work.at[c, 0], r, p + g, tiles)
            put_tile(work.at[c, 1], r, p - g, tiles)
        return e, parts

    def back(r, state):
        e, parts = state
        for c in range(2):
            mine = parts[c]
            f, p, h = mine["f"], mine["p"], parts[1 - c]["h"]
            along_x = tile_of(work.at[c, 0], r, 1) + tile_of(work.at[c, 1], r, -1)
            along_y = lanes_after(p + h) + lanes_before(p - h)
            total = gathered(c, e, mine["sum_x"], mine["sum_y"], along_x, along_y)
            total = total + strip[3, rows_of(r), :] * lanes_before(f, GROUP)
            total = total + strip[4, rows_of(r), :] * lanes_after(f, GROUP)
            if source is not None:
                total = total + source(c, r)
            put_tile(news.at[c], r, keep * f + strip[1 + c, rows_of(r), :] * total, tiles)

    in_turn(tiles, front, back)


def join_sides(sides, left, right, column):
    for r in range(sides.shape[1] // 8):
        for c in range(2):
            both = jnp.where(column == HALO, tile_of(left.at[c], r), tile_of(right.at[c], r))
            sides[c, rows_of(r), :] = both


def join_edges(edges, strips, left, right, column, tiles):
    for r in range(tiles):
        sums = []
        for strip, fields, sign in ((strips[0], left, -1.0), (strips[1], right, 1.0)):
            e = strip[0, rows_of(r), :]
            p, h = [], []
            for c in range(2):
                _, wh = cross_factors(c, e)
                step = tile_of(fields.at[c], r, 1) - tile_of(fields.at[c], r, -1)
                p.append(e * tile_of(fields.at[c], r))
                h.append((sign * wh) * step)
            sums.append([p[c] + h[1 - c] for c in range(2)])
        before = column == HALO - 1
        for c in range(2):
            f = jnp.where(before, tile_of(left.at[c], r), tile_of(right.at[c], r))
            edges[0, c, rows_of(r), :] = f
            edges[1, c, rows_of(r), :] = jnp.where(before, sums[0][c], sums[1][c])


def plane_sweep(k, lane, eta, fields, products, scale, keep, work, put, sides, edges, source=None):
    tiles = scale.shape[2] // 8
    count = tiles if edges is None else tiles - 1
    cols = lane.shape[1]
    back_by = cols - (GROUP * k + HALO)
    first, last = lane == 0, lane == cols - 1
    at_side = first | last

    def front(r):
        e = tile_of(eta.at[k + 1], r)
        parts = []
        for c in range(2):
            plane = fields.at[c, k + 1]
            f = tile_of(plane, r)
            low = high = f
            if edges is not None:
                edge = pltpu.roll(edges[0, c, rows_of(r), :], back_by, 1)
                low, high = jnp.where(last, edge, f), jnp.where(first, edge, f)
            y_low, y_high = lanes_before(low), lanes_after(high)
            x_low, x_high = tile_of(plane, r, -1), tile_of(plane, r, 1)
            wg, wh = cross_factors(c, e)
            part = dict(f=f, g=wg * (y_high - y_low), h=wh * (x_high - x_low))
            part.update(sum_x=x_low + x_high, sum_y=y_low + y_high)
            part.update(p=tile_of(products.at[c, k + 1], r))
            parts.append(part)
        for c in range(2):
            p, g = parts[c]["p"], parts[1 - c]["g"]
            put_tile(work.at[c, 0], r, p + g, tiles)
            put_tile(work.at[c, 1], r, p - g, tiles)
        return e, parts

    def back(r, state):
        e, parts = state
        for c in range(2):
            mine = parts[c]
            p, h = mine["p"], parts[1 - c]["h"]
            low, high = p - h, p + h
            if edges is not None:
                edge = pltpu.roll(edges[1, c, rows_of(r), :], back_by, 1)
                low, high = jnp.where(last, edge, low), jnp.where(first, edge, high)
            along_x = tile_of(work.at[c, 0], r, 1) + tile_of(work.at[c, 1], r, -1)
            along_y = lanes_before(low) + lanes_after(high)
            sum_z = tile_of(fields.at[c, k], r) + tile_of(fields.at[c, k + 2], r)
            p_z = tile_of(products.at[c, k], r) + tile_of(products.at[c, k + 2], r)
            sums = [mine["sum_x"], mine["sum_y"]]
            alongs = [along_x, along_y]
            sums[c], alongs[c] = sums[c] + sum_z, alongs[c] + p_z
            total = gathered(c, e, sums[0], sums[1], alongs[0], alongs[1])
            if source is not None:
                total = total + source(c, r)
            new = keep * mine["f"] + scale[c, k, rows_of(r), :] * total
            if edges is None:
                side = pltpu.roll(sides[c, rows_of(r), :], back_by, 1)
                new = jnp.where(at_side, side, new)
            put(c, k, r, e, new)

    in_turn(tiles, front, back, count)


def inverse_pair(e, e_x, e_y, e_z, ends, basal, cover):
    double = 2.0 * e
    both_x, both_y = e_x + double, e_y + double
    vertical = (VERTICAL / 2) * (e_z + ends * e) + basal
    first = 2.0 * both_x + 0.5 * both_y + vertical
    second = 0.5 * both_x + 2.0 * both_y + vertical
    inverse = cover / jnp.where(cover > 0.0, first * second, 1.0)
    return inverse * second, inverse * first


UNROLL = 1


def over_layers(layers, body):
    def some(i, carry):
        for slot in range(UNROLL):
            body(UNROLL * i + slot, slot)
        return carry

    lax.fori_loop(0, layers // UNROLL, some, 0)
    for k in range(layers // UNROLL * UNROLL, layers):
        body(k, k % UNROLL)


def sweep_kernel(
    layers,
    adj, eta_in, fr, ice, above, below, packed, packed_left, packed_right, basal_velocity,
    out, gradient, carry_out,
    fields, products, eta, cover, friction, eta_edge, sides, edges,
    strip_fields, strip_work, plane_work, circle_work, scale, strips,
):
    circle, cols = friction.shape
    tiles = circle // 8
    lane = lane_index((8, cols))
    column = lane % GROUP
    omegas = omega_list(ITERS)

    whole_column = lane_index((circle, cols)) % GROUP
    for side in range(2):
        values = []
        for field in range(3):
            own = packed[field]
            if side == 0:
                values.append(jnp.where(whole_column < HALO, packed_left[field], own))
            else:
                values.append(jnp.where(whole_column < HALO, own, packed_right[field]))
        strip_planes(strips.at[side], values[2], layers, strip_work.at[side, 0, 0])
        for c in range(2):
            for r in range(tiles):
                put_tile(strip_fields.at[0, side, c], r, values[c][rows_of(r)], tiles)
    for r in range(tiles):
        both = jnp.where(
            column == HALO - 1, strips[0, 0, rows_of(r), :], strips[1, 0, rows_of(r), :]
        )
        eta_edge[rows_of(r), :] = both

    zero = jnp.zeros((stored(circle), cols), F32)
    for end in (0, layers + 1):
        eta[end] = zero
        for half in range(2):
            for c in range(2):
                fields[half, c, end] = zero
                products[half, c, end] = zero
    covered = ice[...] > 0
    extend(friction, fr[...], above, below, 3 * layers)
    for layer in range(layers):
        slot = circle_work.at[layer % 2]
        values = eta_in[layer]
        signed = slot.at[0]
        extend(signed, jnp.where(covered, values, -values), above, below, 2 * layers + layer)
        for c in range(2):
            values = jnp.where(covered, adj[c, layer], 0.0)
            extend(slot.at[1 + c], values, above, below, c * layers + layer)
        for r in range(tiles):
            here = signed[rows_of(r), :]
            if layer == 0:
                cover[rows_of(r), :] = jnp.where(here > 0.0, 2.0, 0.0)
            e = jnp.abs(here)
            put_tile(eta.at[layer + 1], r, e, tiles)
            for c in range(2):
                f = slot[1 + c, rows_of(r), :]
                put_tile(fields.at[0, c, layer + 1], r, f, tiles)
                products[0, c, layer + 1, LEAD + 8 * r : LEAD + 8 * (r + 1), :] = e * f

    def weigh(k, slot):
        is_end = (k == 0) | (k == layers - 1)
        ends = jnp.where(is_end, 1.0, 2.0)
        lowest = jnp.where(k == layers - 1, 1.0, 0.0)
        plane = eta.at[k + 1]
        for r in range(tiles):
            e = tile_of(plane, r)
            edge = pltpu.roll(eta_edge[rows_of(r), :], cols - (GROUP * k + HALO), 1)
            e_y = lanes_before(jnp.where(lane == cols - 1, edge, e))
            e_y = e_y + lanes_after(jnp.where(lane == 0, edge, e))
            pair = inverse_pair(
                e,
                tile_of(plane, r, -1) + tile_of(plane, r, 1),
                e_y,
                tile_of(eta.at[k], r) + tile_of(eta.at[k + 2], r),
                ends,
                lowest * friction[rows_of(r), :],
                cover[rows_of(r), :],
            )
            scale[0, k, rows_of(r), :], scale[1, k, rows_of(r), :] = pair

    over_layers(layers, weigh)

    total = math.prod(omegas)
    for turn, omega in enumerate(omegas):
        final = turn == ITERS - 1
        half = turn % 2
        olds = strip_fields.at[half]
        news = strip_fields.at[1 - half]
        keep = keep_of(omega)
        if final:
            join_edges(
                edges, (strips.at[0], strips.at[1]), olds.at[0], olds.at[1], column, tiles - 1 + 1
            )
        else:
            for side in range(2):
                strip_sweep(
                    strips.at[side], olds.at[side], news.at[side], keep, strip_work.at[side]
                )
            join_sides(sides, news.at[0], news.at[1], column)

        def put(c, k, r, e, new, final=final, half=half):
            if final:
                out[c, k, rows_of(r), :] = total * new
            else:
                put_tile(fields.at[1 - half, c, k + 1], r, new, tiles)
                products[1 - half, c, k + 1, LEAD + 8 * r : LEAD + 8 * (r + 1), :] = e * new

        def sweep(k, slot, final=final, half=half, keep=keep, put=put):
            plane_sweep(
                k, lane, eta, fields.at[half], products.at[half], scale, keep,
                plane_work.at[slot], put, sides, edges if final else None,
            )

        over_layers(layers, sweep)

    flow = basal_velocity[0] * out[0, layers - 1] + basal_velocity[1] * out[1, layers - 1]
    gradient[...] = jnp.where(covered, -fr[...] * flow, 0.0)
    for i in range(2):
        for k in range(ITERS):
            carry_out[i, k] = scale[i, k]
        for k in range(3):
            carry_out[i, ITERS + k] = strips[i, k]
        for k in range(2):
            carry_out[i, ITERS + 3 + k] = eta[2 * i + k + 1, LEAD : LEAD + circle, :]


def free_sweeps(adjoint, viscosity, friction, ice_mask, edges, packed, basal_velocity):
    _, layers, rows, cols = adjoint.shape
    circle = rows + 8
    plane = (circle, cols)
    kept = (stored(circle), cols)
    stack = (layers + 2,) + kept
    return pl.pallas_call(
        functools.partial(sweep_kernel, layers),
        in_specs=vmem_specs(10),
        out_specs=vmem_specs(3),
        out_shape=[
            jax.ShapeDtypeStruct(adjoint.shape, F32),
            jax.ShapeDtypeStruct((rows, cols), F32),
            jax.ShapeDtypeStruct((2, ITERS + 5) + plane, F32),
        ],
        scratch_shapes=[
            pltpu.VMEM((2, 2) + stack, F32),
            pltpu.VMEM((2, 2) + stack, F32),
            pltpu.VMEM(stack, F32),
            pltpu.VMEM(plane, F32),
            pltpu.VMEM(plane, F32),
            pltpu.VMEM(plane, F32),
            pltpu.VMEM((2,) + plane, F32),
            pltpu.VMEM((2, 2) + plane, F32),
            pltpu.VMEM((2, 2, 2) + kept, F32),
            pltpu.VMEM((2, 2, 2) + kept, F32),
            pltpu.VMEM((UNROLL, 2, 2) + kept, F32),
            pltpu.VMEM((2, 3) + plane, F32),
            pltpu.VMEM((2, layers) + plane, F32),
            pltpu.VMEM((2, 5) + plane, F32),
        ],
        compiler_params=pltpu.CompilerParams(vmem_limit_bytes=24 << 20),
        cost_estimate=pl.CostEstimate(
            flops=200_000_000, transcendentals=0, bytes_accessed=8_000_000
        ),
        name="free_sweeps",
    )(adjoint, viscosity, friction, ice_mask, *edges, *packed, basal_velocity)


EXTRA = 12
CORNER = 16


def pack_kernel(capacity, tile_in, row_in, misfit_in, out, keys_out, counts_out,
                tile, row, misfit, slot_vector, slot, sems):
    copies = [
        pltpu.make_async_copy(source, target, sems.at[i])
        for i, (source, target) in enumerate(
            ((tile_in, tile), (row_in, row), (misfit_in, misfit))
        )
    ]
    for copy in copies:
        copy.start()
    turns, lanes = tile.shape
    devices = keys_out.shape[0]
    device = lax.broadcasted_iota(jnp.int32, (devices, lanes), 0)
    at_row = lax.broadcasted_iota(jnp.int32, (lanes, lanes), 0)
    at_lane = lax.broadcasted_iota(jnp.int32, (lanes, lanes), 1)
    earlier = jnp.where(at_row < at_lane, 1.0, 0.0).astype(BF16)
    copies[0].wait()
    seen = jnp.zeros((devices, 1), F32)
    onehots, ranks = [], []
    for turn in range(turns):
        target = tile[turn : turn + 1, :]
        onehot = jnp.where(device == target, 1.0, 0.0)
        before = jnp.dot(onehot.astype(BF16), earlier, preferred_element_type=F32) + seen
        rank = jnp.sum(onehot * before, axis=0, keepdims=True).astype(jnp.int32)
        slot_vector[turn : turn + 1, :] = target * capacity + rank
        seen = seen + jnp.sum(onehot, axis=1, keepdims=True)
        onehots.append(onehot)
        ranks.append(rank)
    copy = pltpu.make_async_copy(slot_vector, slot, sems.at[3])
    copy.start()
    counts_out[...] = jnp.broadcast_to(seen, counts_out.shape)
    copies[1].wait()
    keys = jnp.zeros((devices, lanes), F32)
    for turn in range(turns):
        named = onehots[turn] * (row[turn : turn + 1, :] + 1).astype(F32)
        place = jnp.where(at_row // 2 == ranks[turn], 1.0, 0.0).astype(BF16)
        keys = keys + lax.dot_general(
            named.astype(BF16), place, (((1,), (1,)), ((), ())), preferred_element_type=F32
        )
    keys_out[...] = keys
    copies[2].wait()
    copy.wait()

    def place_row(turn, carry):
        for i in range(lanes):
            out[slot[turn, i]] = misfit[turn * lanes + i]
        return carry

    lax.fori_loop(0, turns, place_row, 0)


def pack_blocks(misfit, block_tile, block_row, devices, capacity):
    count, _, cols = misfit.shape
    grid_shape = (count // cols, cols)
    return pl.pallas_call(
        functools.partial(pack_kernel, capacity),
        in_specs=[pl.BlockSpec(memory_space=pltpu.HBM)] * 3,
        out_specs=vmem_specs(3),
        out_shape=[
            jax.ShapeDtypeStruct((devices * capacity, 2, cols), BF16),
            jax.ShapeDtypeStruct((devices, cols), F32),
            jax.ShapeDtypeStruct((devices, cols), F32),
        ],
        scratch_shapes=[
            pltpu.VMEM(grid_shape, jnp.int32),
            pltpu.VMEM(grid_shape, jnp.int32),
            pltpu.VMEM(misfit.shape, BF16),
            pltpu.VMEM(grid_shape, jnp.int32),
            pltpu.SMEM(grid_shape, jnp.int32),
            pltpu.SemaphoreType.DMA((4,)),
        ],
        compiler_params=pltpu.CompilerParams(vmem_limit_bytes=4 << 20),
        name="pack_blocks",
    )(block_tile.reshape(grid_shape), block_row.reshape(grid_shape), misfit)


def wanted_of(keys, rows):
    odd = lax.broadcasted_iota(jnp.int32, keys.shape, 1) % 2
    return jnp.where(keys > 0.0, keys - 1.0 + odd.astype(F32) * rows, -1.0)


def halves(values):
    high = values.astype(BF16).astype(F32)
    return jnp.concatenate([high, values - high], axis=0)


def bundle_kernel(devices, across, capacity, rows, slots, keys, counts, out, upper, lower, column):
    lanes = slots.shape[1]
    span = 2 * capacity
    place = span + 2 * EXTRA
    at_row = lax.broadcasted_iota(jnp.int32, (span, lanes), 0).astype(F32)
    line = lax.broadcasted_iota(jnp.int32, (8, lanes), 0)
    lane = lax.broadcasted_iota(jnp.int32, (8, lanes), 1)
    ends = jnp.where(line < 4, rows - 2, 0) + (line // 2 % 2) * rows + line % 2
    ends = ends[:, :span].astype(F32)
    pick = (line == 1) & (lane == lanes - 2) | (line == 2) & (lane == lanes - 1)
    pick = pick | (line == 3) & (lane == 0) | (line == 4) & (lane == 1)
    pick = jnp.where(pick, 1.0, 0.0).astype(BF16)
    for t in range(devices):
        used = 2.0 * counts[t : t + 1, :]
        block = slots[span * t : span * (t + 1), :].astype(F32)
        block = jnp.where(at_row < used, block, 0.0).astype(BF16)
        out[place * t : place * t + span, :] = block
        wanted = wanted_of(keys[t : t + 1, :], rows)[:, :span]
        select = jnp.where(ends == wanted, 1.0, 0.0).astype(BF16)
        found = jnp.dot(select, block, preferred_element_type=F32)
        upper[t] = halves(found[:4])
        lower[t] = halves(found[4:])
        side = lax.dot_general(
            pick, block, (((1,), (1,)), ((), ())), preferred_element_type=F32
        )
        if span < lanes:
            side = jnp.concatenate([side, jnp.zeros((8, lanes - span), F32)], axis=1)
        column[t] = side
    zero_row = jnp.zeros((1, lanes), F32)
    zero_edge = jnp.zeros((8, lanes), F32)
    for t in range(devices):
        has_left, has_right = t % across > 0, t % across < across - 1
        has_above, has_below = t >= across, t < devices - across
        above = upper[t - across] if has_above else zero_edge
        below = lower[t + across] if has_below else zero_edge
        corner = zero_edge
        for near, there, edge, first in (
            (t - across, has_above, upper, 0),
            (t + across, has_below, lower, 8),
        ):
            if there and has_left:
                value = pltpu.roll(edge[near - 1], HALO + first, 1)
                corner = jnp.where((lane == first + 1) | (lane == first + 2), value, corner)
            if there and has_right:
                value = pltpu.roll(edge[near + 1], HALO + first, 1)
                corner = jnp.where((lane == first + 3) | (lane == first + 4), value, corner)
        corner = pltpu.roll(corner, 0, 1, stride=CORNER, stride_axis=0)
        corner = jnp.sum(corner, axis=0, keepdims=True)
        key_left = keys[t - 1 : t, :] if has_left else zero_row
        key_right = keys[t + 1 : t + 2, :] if has_right else zero_row
        left = column[t - 1, 1:3, :] if has_left else zero_edge[:2]
        right = column[t + 1, 3:5, :] if has_right else zero_edge[:2]
        head = jnp.concatenate(
            [keys[t : t + 1, :], key_left, key_right, corner, left, right], axis=0
        )
        extra = jnp.concatenate([head, above, below], axis=0).astype(BF16)
        out[place * t + span : place * (t + 1), :] = extra


def bundle_blocks(slots, keys, counts, across, capacity, rows):
    devices, cols = keys.shape
    length = devices * 2 * (capacity + EXTRA)
    edge = pltpu.VMEM((devices, 8, cols), F32)
    return pl.pallas_call(
        functools.partial(bundle_kernel, devices, across, capacity, rows),
        in_specs=vmem_specs(3),
        out_specs=pl.BlockSpec(memory_space=pltpu.VMEM),
        out_shape=jax.ShapeDtypeStruct((length, cols), BF16),
        scratch_shapes=[edge, edge, edge],
        compiler_params=pltpu.CompilerParams(vmem_limit_bytes=8 << 20),
        name="bundle_blocks",
    )(slots, keys, counts)


def source_of(devices, capacity, rows, got, source, beside):
    lanes = got.shape[1]
    circle = rows + 8
    span = 2 * capacity
    place = span + 2 * EXTRA
    group = max(1, lanes // span)
    at_row = lax.broadcasted_iota(jnp.int32, (2 * rows, lanes), 0).astype(F32)
    line = lax.broadcasted_iota(jnp.int32, (8, lanes), 0)
    total = jnp.zeros((2 * rows, lanes), F32)
    side = jnp.zeros((2 * rows, 8), F32)
    extra_sum = jnp.zeros((2 * EXTRA, lanes), F32)
    contract = (((1,), (1,)), ((), ()))
    pair_pick, pair_block = [], []
    for first in range(0, devices, group):
        keys, blocks = None, []
        for q in range(group):
            start = (first + q) * place
            extra = got[start + span : start + place, :].astype(F32)
            extra_sum = extra_sum + extra
            head = pltpu.roll(extra[:8], q * span, 1) if q else extra[:8]
            keys = head if keys is None else keys + head
            blocks.append(got[start : start + span, :])
        wanted = wanted_of(keys[:3], rows)
        block = blocks[0] if group == 1 else jnp.concatenate(blocks, axis=0)
        picks = [
            jnp.where(at_row == wanted[i : i + 1], 1.0, 0.0).astype(BF16) for i in range(3)
        ]
        pair_pick.append(picks[0])
        pair_block.append(block)
        if len(pair_pick) == 2:
            pick, block = jnp.concatenate(pair_pick, axis=1), jnp.concatenate(pair_block, axis=0)
            total = total + jnp.dot(pick, block, preferred_element_type=F32)
            pair_pick, pair_block = [], []
        low = jnp.where((line == 1) | (line == 2), pltpu.roll(keys, 5, 0), 0.0).astype(BF16)
        high = jnp.where((line == 3) | (line == 4), pltpu.roll(keys, 5, 0), 0.0).astype(BF16)
        pick, both = jnp.concatenate(picks[1:], axis=1), jnp.concatenate([low, high], axis=1)
        side = side + lax.dot_general(pick, both, contract, preferred_element_type=F32)
    above = extra_sum[8:12] + extra_sum[12:16]
    below = extra_sum[16:20] + extra_sum[20:24]
    lane = lax.broadcasted_iota(jnp.int32, (8, lanes), 1)
    corner = jnp.where(lane // CORNER == 7 - line, extra_sum[3:4], 0.0)
    corner = pltpu.roll(corner, lanes - 7 * CORNER, 1, stride=CORNER, stride_axis=0)
    corner = corner[:4] + corner[4:]
    corner = jnp.concatenate([corner[3 - i : 4 - i] for i in range(4)], axis=0)
    corner_below = pltpu.roll(corner, lanes - 8, 1)
    side = jnp.concatenate([side, jnp.zeros((2 * rows, lanes - 8), F32)], axis=1)
    gap = jnp.zeros((4, lanes), F32)
    for c in range(2):
        for target, inner, after, before in (
            (source, total, below, above),
            (beside, side, corner_below, corner),
        ):
            target[c, :rows, :] = inner[c * rows : (c + 1) * rows]
            target[c, rows : rows + 2, :] = after[2 * c : 2 * c + 2]
            target[c, rows + 2 : circle - 2, :] = gap
            target[c, circle - 2 : circle, :] = before[2 * c : 2 * c + 2]


def response_kernel(
    devices, capacity,
    got, scale, adj_in,
    out, source, beside, fields, products, eta, sides, edges,
    drives, strip_fields, strip_work, plane_work, strips,
):
    circle, cols = source.shape[1:]
    rows = out.shape[2]
    tiles = circle // 8
    source_of(devices, capacity, rows, got, source, beside)
    lane = lane_index((8, cols))
    column = lane % GROUP
    omegas = omega_list(ITERS)
    zero = jnp.zeros((stored(circle), cols), F32)
    top = lane < GROUP
    for side in range(2):
        for r in range(tiles):
            e = scale[side, ITERS, rows_of(r), :]
            for i in range(3):
                strips[side, i, rows_of(r), :] = scale[side, ITERS + i, rows_of(r), :]
            strips[side, 3, rows_of(r), :] = e + lanes_before(e, GROUP)
            strips[side, 4, rows_of(r), :] = e + lanes_after(e, GROUP)
    for k in range(2):
        for half in range(2):
            for c in range(2):
                fields[half, c, 0] = zero
                products[half, c, 0] = zero
                fields[half, c, 2 + half + k] = zero
                products[half, c, 2 + half + k] = zero
    eta[0] = zero
    for k in range(ITERS + 1):
        for r in range(tiles):
            put_tile(eta.at[k + 1], r, scale[k // 2, ITERS + 3 + k % 2, rows_of(r), :], tiles)

    def put_strip(turn, side, c, r, value):
        put_tile(strip_fields.at[turn % 2, side, c], r, value, tiles)

    for r in range(tiles):
        e = tile_of(eta.at[1], r)
        for c in range(2):
            drive = 0.5 * source[c, rows_of(r), :]
            source[c, rows_of(r), :] = drive
            f = scale[c, 0, rows_of(r), :] * drive
            put_tile(fields.at[0, c, 1], r, f, tiles)
            products[0, c, 1, LEAD + 8 * r : LEAD + 8 * (r + 1), :] = e * f
            own = lanes_before(drive, HALO)
            near = 0.5 * beside[c, rows_of(r), :]
            for side in range(2):
                pair = (near, own) if side == 0 else (own, near)
                both = jnp.where(top, jnp.where(column < HALO, pair[0], pair[1]), 0.0)
                drives[side, c, rows_of(r), :] = both
                put_strip(0, side, c, r, strips[side, 1 + c, rows_of(r), :] * both)

    reach = omegas[0]
    for turn in range(1, ITERS):
        final = turn == ITERS - 1
        half = turn - 1
        part = 1.0 / reach
        keep = keep_of(omegas[turn])
        olds, news = strip_fields.at[half % 2], strip_fields.at[turn % 2]
        if final:
            join_edges(
                edges, (strips.at[0], strips.at[1]), olds.at[0], olds.at[1], column, tiles
            )
        else:
            for side in range(2):
                strip_sweep(
                    strips.at[side], olds.at[side], news.at[side], keep, strip_work.at[side],
                    lambda c, r, side=side: part * drives[side, c, rows_of(r), :],
                )
            join_sides(sides, news.at[0], news.at[1], column)
        after = reach * omegas[turn]

        def put(c, k, r, e, new, final=final, turn=turn, after=after):
            if final:
                out[c, k, rows_of(r), :] = adj_in[c, k, rows_of(r), :] + after * new
            else:
                put_tile(fields.at[turn, c, k + 1], r, new, tiles)
                products[turn, c, k + 1, LEAD + 8 * r : LEAD + 8 * (r + 1), :] = e * new

        for k in range(turn + 1):
            drive = None
            if k == 0:
                drive = lambda c, r, part=part: part * source[c, rows_of(r), :]
            plane_sweep(
                k, lane, eta, fields.at[half], products.at[half], scale, keep,
                plane_work.at[k % 2], put, sides, edges if final else None, drive,
            )
        reach = after


def add_response(got, devices, capacity, carry, adjoint):
    circle, cols = carry.shape[2:]
    _, _, rows, _ = adjoint.shape
    plane = (circle, cols)
    kept = (stored(circle), cols)
    top = pl.BlockSpec((2, ITERS, rows, cols), lambda i: (0, 0, 0, 0))

    def whole(array):
        return pl.BlockSpec(array.shape, lambda i, n=array.ndim: (0,) * n)

    return pl.pallas_call(
        functools.partial(response_kernel, devices, capacity),
        grid=(1,),
        in_specs=[whole(got), whole(carry), top],
        out_specs=top,
        out_shape=jax.ShapeDtypeStruct(adjoint.shape, F32),
        scratch_shapes=[
            pltpu.VMEM((2,) + plane, F32),
            pltpu.VMEM((2,) + plane, F32),
            pltpu.VMEM((2, 2, ITERS + 2) + kept, F32),
            pltpu.VMEM((2, 2, ITERS + 2) + kept, F32),
            pltpu.VMEM((ITERS + 2,) + kept, F32),
            pltpu.VMEM((2,) + plane, F32),
            pltpu.VMEM((2, 2) + plane, F32),
            pltpu.VMEM((2, 2) + plane, F32),
            pltpu.VMEM((2, 2, 2) + kept, F32),
            pltpu.VMEM((2, 2, 2) + kept, F32),
            pltpu.VMEM((2, 2, 2) + kept, F32),
            pltpu.VMEM((2, 5) + plane, F32),
        ],
        input_output_aliases={2: 0},
        compiler_params=pltpu.CompilerParams(vmem_limit_bytes=12 << 20),
        name="add_response",
    )(got, carry, adjoint)


def on_device(
    adjoint_prev, viscosity, friction, basal_velocity, ice_mask, misfit, block_tile, block_row
):
    devices = lax.axis_size("gx") * lax.axis_size("gy")
    layers, rows, cols = adjoint_prev.shape[1:]
    capacity = 2 * misfit.shape[0] // devices
    assert layers > 2 * ITERS and GROUP * (layers + 1) <= cols and rows % 8 == 0
    assert devices % (cols // capacity) == 0 and 2 * capacity <= cols and cols % (2 * capacity) == 0 and misfit.shape[0] % cols == 0

    edge_low, edge_high = edge_rows(adjoint_prev, viscosity, friction, ice_mask)
    above = shift_up(edge_high, "gx")
    below = shift_down(edge_low, "gx")
    slots, keys, counts = pack_blocks(misfit, block_tile, block_row, devices, capacity)
    sent = bundle_blocks(
        slots.reshape(-1, cols), keys, counts, lax.axis_size("gy"), capacity, rows
    )
    got = lax.all_to_all(
        sent.reshape(devices, -1, cols), ("gx", "gy"), split_axis=0, concat_axis=0, tiled=True
    )
    packed = edge_columns(adjoint_prev, viscosity, friction, ice_mask, above, below)
    left = shift_up(packed, "gy")
    right = shift_down(packed, "gy")
    adjoint, gradient, carry = free_sweeps(
        adjoint_prev, viscosity, friction, ice_mask, (above, below), (packed, left, right),
        basal_velocity,
    )
    adjoint = add_response(
        got.reshape(-1, cols), devices, capacity, carry, adjoint
    )
    return (adjoint, gradient)


def solution(mesh):
    placed = (
        P(None, None, "gx", "gy"),
        P(None, "gx", "gy"),
        P("gx", "gy"),
        P(None, "gx", "gy"),
        P("gx", "gy"),
        P(("gx", "gy"), None, None),
        P(("gx", "gy"), None),
        P(("gx", "gy")),
    )

    return jax.shard_map(
        on_device,
        mesh=mesh,
        in_specs=placed,
        out_specs=(P(None, None, "gx", "gy"), P("gx", "gy")),
        check_vma=False,
    )
```

```python
import functools
import math

import jax
import jax.numpy as jnp
from jax import lax
from jax.experimental import pallas as pl
from jax.experimental.pallas import tpu as pltpu
from jax.sharding import PartitionSpec as P


ITERS = 3
HALO = ITERS
GROUP = 2 * HALO
VERTICAL = 4.0

F32 = jnp.float32
BF16 = jnp.bfloat16


def omega_list(count):
    return [
        1.0 / (1.3 + 1.2 * math.cos((2 * turn_id + 1) * math.pi / (2 * count)))
        for turn_id in range(count)
    ]


def shift_up(array, axis):
    peers = lax.axis_size(axis)
    return lax.ppermute(array, axis, [(i, i + 1) for i in range(peers - 1)])


def shift_down(array, axis):
    peers = lax.axis_size(axis)
    return lax.ppermute(array, axis, [(i + 1, i) for i in range(peers - 1)])


def vmem_specs(count):
    return [pl.BlockSpec(memory_space=pltpu.VMEM) for _ in range(count)]


LEAD = 8


def stored(circle):
    return circle + 2 * LEAD


def tile_of(ref, r, step=0):
    return ref[LEAD + 8 * r + step : LEAD + 8 * (r + 1) + step, :]


def put_tile(ref, r, values, tiles):
    ref[LEAD + 8 * r : LEAD + 8 * (r + 1), :] = values
    if r == tiles - 1:
        ref[LEAD - 1 : LEAD, :] = values[7:, :]
    if r == 0:
        ref[LEAD + 8 * tiles : LEAD + 8 * tiles + 1, :] = values[:1, :]


def rows_of(r):
    return slice(8 * r, 8 * (r + 1))


def lanes_before(values, step=1):
    return pltpu.roll(values, step, 1)


def lanes_after(values, step=1):
    return pltpu.roll(values, values.shape[1] - step, 1)


def lane_index(shape):
    return lax.broadcasted_iota(jnp.int32, shape, len(shape) - 1)


def extend(slot, values, above, below, plane):
    rows = values.shape[0]
    circle = slot.shape[0]
    first = HALO * plane
    slot[:rows, :] = values
    slot[rows : rows + HALO, :] = below[first : first + HALO, :]
    slot[rows + HALO : circle - HALO, :] = jnp.zeros((8 - 2 * HALO, values.shape[1]), F32)
    slot[circle - HALO : circle, :] = above[first : first + HALO, :]
    return slot


def in_turn(tiles, front, back, count=None):
    done = {tiles - 1: front(tiles - 1), 0: front(0)}
    count = tiles if count is None else count
    for r in range(1, tiles - 1):
        done[r] = front(r)
        back(r - 1, done[r - 1])
    for r in range(tiles - 2, count):
        back(r, done[r])


def edge_kernel(layers, adj_lo, adj_hi, eta_lo, eta_hi, fr_lo, fr_hi, ice_lo, ice_hi, lo, hi):
    for adj, eta, fr, ice, out, at in (
        (adj_lo, eta_lo, fr_lo, ice_lo, lo, 0),
        (adj_hi, eta_hi, fr_hi, ice_hi, hi, 8 - HALO),
    ):
        rows = slice(at, at + HALO)
        covered = ice[rows, :] > 0
        for plane in range(2 * layers):
            values = jnp.where(covered, adj[plane // layers, plane % layers, rows, :], 0.0)
            out[HALO * plane : HALO * (plane + 1), :] = values
        for layer in range(layers):
            values = eta[layer, rows, :]
            first = HALO * (2 * layers + layer)
            out[first : first + HALO, :] = jnp.where(covered, values, -values)
        first = HALO * 3 * layers
        out[first : first + HALO, :] = fr[rows, :]


def edge_rows(adjoint, viscosity, friction, ice_mask):
    _, layers, rows, cols = adjoint.shape
    last = rows // 8 - 1
    length = -(-HALO * (3 * layers + 1) // 8) * 8

    def pair(block, index):
        return [
            pl.BlockSpec(block, functools.partial(index, 0)),
            pl.BlockSpec(block, functools.partial(index, last)),
        ]

    specs = pair((2, layers, 8, cols), lambda r, i: (0, 0, r, 0))
    specs += pair((layers, 8, cols), lambda r, i: (0, r, 0))
    specs += pair((8, cols), lambda r, i: (r, 0))
    specs += pair((8, cols), lambda r, i: (r, 0))
    return pl.pallas_call(
        functools.partial(edge_kernel, layers),
        grid=(1,),
        in_specs=specs,
        out_specs=[pl.BlockSpec((length, cols), lambda i: (0, 0))] * 2,
        out_shape=[jax.ShapeDtypeStruct((length, cols), F32)] * 2,
        compiler_params=pltpu.CompilerParams(vmem_limit_bytes=60 << 20),
        name="edge_rows",
    )(adjoint, adjoint, viscosity, viscosity, friction, friction, ice_mask, ice_mask)


def column_kernel(layers, adj, eta, fr, ice, above, below, packed, work):
    rows, cols = fr.shape
    circle = rows + 8
    lane_layer = lane_index((circle, cols)) // GROUP
    covered = ice[...] > 0

    def gather(total, values, layer):
        return jnp.where(
            lane_layer == layer, pltpu.roll(values, (HALO + GROUP * layer) % cols, 1), total
        )

    for field in range(3):
        total = jnp.zeros((circle, cols), F32)
        for layer in range(layers):
            if field == 2:
                values = jnp.where(covered, eta[layer], -eta[layer])
            else:
                values = jnp.where(covered, adj[field, layer], 0.0)
            slot = extend(work.at[layer % 2], values, above, below, field * layers + layer)
            total = gather(total, slot[...], layer)
        if field == 2:
            slot = extend(work.at[layers % 2], fr[...], above, below, 3 * layers)
            total = gather(total, slot[...], layers)
        packed[field] = total


def edge_columns(adjoint, viscosity, friction, ice_mask, above, below):
    _, layers, rows, cols = adjoint.shape
    circle = rows + 8
    return pl.pallas_call(
        functools.partial(column_kernel, layers),
        in_specs=vmem_specs(6),
        out_specs=pl.BlockSpec(memory_space=pltpu.VMEM),
        out_shape=jax.ShapeDtypeStruct((3, circle, cols), F32),
        scratch_shapes=[pltpu.VMEM((2, circle, cols), F32)],
        compiler_params=pltpu.CompilerParams(vmem_limit_bytes=4 << 20),
        name="edge_columns",
    )(adjoint, viscosity, friction, ice_mask, above, below)


def keep_of(omega):
    return (1.0 - omega) / omega


def cross_factors(c, e):
    half, quarter = 0.5 * e, 0.25 * e
    return (half, quarter) if c == 0 else (quarter, half)


def gathered(c, e, sum_x, sum_y, along_x, along_y):
    strong, weak = (0, 1) if c == 0 else (1, 0)
    sums, alongs = (sum_x, sum_y), (along_x, along_y)
    return e * (sums[strong] + 0.25 * sums[weak]) + (alongs[strong] + 0.25 * alongs[weak])


def strip_planes(strip, signed, layers, scratch):
    circle, cols = signed.shape
    tiles = circle // 8
    lane = lane_index((8, cols))
    inside = lane < GROUP * layers
    bottom = inside & (lane >= GROUP * (layers - 1))
    ends = jnp.where(bottom | (lane < GROUP), 1.0, 2.0)
    for r in range(tiles):
        e = jnp.where(inside, jnp.abs(signed[rows_of(r)]), 0.0)
        put_tile(scratch, r, e, tiles)
        strip[0, rows_of(r), :] = e
    for r in range(tiles):
        e = tile_of(scratch, r)
        here = signed[rows_of(r)]
        z_low, z_high = lanes_before(e, GROUP), lanes_after(e, GROUP)
        strip[3, rows_of(r), :] = e + z_low
        strip[4, rows_of(r), :] = e + z_high
        pair = inverse_pair(
            e,
            tile_of(scratch, r, -1) + tile_of(scratch, r, 1),
            lanes_before(e) + lanes_after(e),
            z_low + z_high,
            ends,
            jnp.where(bottom, lanes_after(here, GROUP), 0.0),
            jnp.where(inside & (here > 0.0), 2.0, 0.0),
        )
        strip[1, rows_of(r), :], strip[2, rows_of(r), :] = pair


def strip_sweep(strip, fields, news, keep, work, source=None):
    tiles = strip.shape[1] // 8

    def front(r):
        e = strip[0, rows_of(r), :]
        parts = []
        for c in range(2):
            f = tile_of(fields.at[c], r)
            y_low, y_high = lanes_before(f), lanes_after(f)
            x_low, x_high = tile_of(fields.at[c], r, -1), tile_of(fields.at[c], r, 1)
            wg, wh = cross_factors(c, e)
            part = dict(f=f, p=e * f, g=wg * (y_high - y_low), h=wh * (x_high - x_low))
            part.update(sum_x=x_low + x_high, sum_y=y_low + y_high)
            parts.append(part)
        for c in range(2):
            p, g = parts[c]["p"], parts[1 - c]["g"]
            put_tile(work.at[c, 0], r, p + g, tiles)
            put_tile(work.at[c, 1], r, p - g, tiles)
        return e, parts

    def back(r, state):
        e, parts = state
        for c in range(2):
            mine = parts[c]
            f, p, h = mine["f"], mine["p"], parts[1 - c]["h"]
            along_x = tile_of(work.at[c, 0], r, 1) + tile_of(work.at[c, 1], r, -1)
            along_y = lanes_after(p + h) + lanes_before(p - h)
            total = gathered(c, e, mine["sum_x"], mine["sum_y"], along_x, along_y)
            total = total + strip[3, rows_of(r), :] * lanes_before(f, GROUP)
            total = total + strip[4, rows_of(r), :] * lanes_after(f, GROUP)
            if source is not None:
                total = total + source(c, r)
            put_tile(news.at[c], r, keep * f + strip[1 + c, rows_of(r), :] * total, tiles)

    in_turn(tiles, front, back)


def join_sides(sides, left, right, column):
    for r in range(sides.shape[1] // 8):
        for c in range(2):
            both = jnp.where(column == HALO, tile_of(left.at[c], r), tile_of(right.at[c], r))
            sides[c, rows_of(r), :] = both


def join_edges(edges, strips, left, right, column, tiles):
    for r in range(tiles):
        sums = []
        for strip, fields, sign in ((strips[0], left, -1.0), (strips[1], right, 1.0)):
            e = strip[0, rows_of(r), :]
            p, h = [], []
            for c in range(2):
                _, wh = cross_factors(c, e)
                step = tile_of(fields.at[c], r, 1) - tile_of(fields.at[c], r, -1)
                p.append(e * tile_of(fields.at[c], r))
                h.append((sign * wh) * step)
            sums.append([p[c] + h[1 - c] for c in range(2)])
        before = column == HALO - 1
        for c in range(2):
            f = jnp.where(before, tile_of(left.at[c], r), tile_of(right.at[c], r))
            edges[0, c, rows_of(r), :] = f
            edges[1, c, rows_of(r), :] = jnp.where(before, sums[0][c], sums[1][c])


def plane_sweep(k, lane, eta, fields, products, scale, keep, work, put, sides, edges, source=None):
    tiles = scale.shape[2] // 8
    count = tiles if edges is None else tiles - 1
    cols = lane.shape[1]
    back_by = cols - (GROUP * k + HALO)
    first, last = lane == 0, lane == cols - 1
    at_side = first | last

    def front(r):
        e = tile_of(eta.at[k + 1], r)
        parts = []
        for c in range(2):
            plane = fields.at[c, k + 1]
            f = tile_of(plane, r)
            low = high = f
            if edges is not None:
                edge = pltpu.roll(edges[0, c, rows_of(r), :], back_by, 1)
                low, high = jnp.where(last, edge, f), jnp.where(first, edge, f)
            y_low, y_high = lanes_before(low), lanes_after(high)
            x_low, x_high = tile_of(plane, r, -1), tile_of(plane, r, 1)
            wg, wh = cross_factors(c, e)
            part = dict(f=f, g=wg * (y_high - y_low), h=wh * (x_high - x_low))
            part.update(sum_x=x_low + x_high, sum_y=y_low + y_high)
            part.update(p=tile_of(products.at[c, k + 1], r))
            parts.append(part)
        for c in range(2):
            p, g = parts[c]["p"], parts[1 - c]["g"]
            put_tile(work.at[c, 0], r, p + g, tiles)
            put_tile(work.at[c, 1], r, p - g, tiles)
        return e, parts

    def back(r, state):
        e, parts = state
        for c in range(2):
            mine = parts[c]
            p, h = mine["p"], parts[1 - c]["h"]
            low, high = p - h, p + h
            if edges is not None:
                edge = pltpu.roll(edges[1, c, rows_of(r), :], back_by, 1)
                low, high = jnp.where(last, edge, low), jnp.where(first, edge, high)
            along_x = tile_of(work.at[c, 0], r, 1) + tile_of(work.at[c, 1], r, -1)
            along_y = lanes_before(low) + lanes_after(high)
            sum_z = tile_of(fields.at[c, k], r) + tile_of(fields.at[c, k + 2], r)
            p_z = tile_of(products.at[c, k], r) + tile_of(products.at[c, k + 2], r)
            sums = [mine["sum_x"], mine["sum_y"]]
            alongs = [along_x, along_y]
            sums[c], alongs[c] = sums[c] + sum_z, alongs[c] + p_z
            total = gathered(c, e, sums[0], sums[1], alongs[0], alongs[1])
            if source is not None:
                total = total + source(c, r)
            new = keep * mine["f"] + scale[c, k, rows_of(r), :] * total
            if edges is None:
                side = pltpu.roll(sides[c, rows_of(r), :], back_by, 1)
                new = jnp.where(at_side, side, new)
            put(c, k, r, e, new)

    in_turn(tiles, front, back, count)


def inverse_pair(e, e_x, e_y, e_z, ends, basal, cover):
    double = 2.0 * e
    both_x, both_y = e_x + double, e_y + double
    vertical = (VERTICAL / 2) * (e_z + ends * e) + basal
    first = 2.0 * both_x + 0.5 * both_y + vertical
    second = 0.5 * both_x + 2.0 * both_y + vertical
    inverse = cover / jnp.where(cover > 0.0, first * second, 1.0)
    return inverse * second, inverse * first


UNROLL = 1


def over_layers(layers, body):
    def some(i, carry):
        for slot in range(UNROLL):
            body(UNROLL * i + slot, slot)
        return carry

    lax.fori_loop(0, layers // UNROLL, some, 0)
    for k in range(layers // UNROLL * UNROLL, layers):
        body(k, k % UNROLL)


def sweep_kernel(
    layers,
    adj, eta_in, fr, ice, above, below, packed, packed_left, packed_right, basal_velocity,
    out, gradient, carry_out,
    fields, products, eta, cover, friction, eta_edge, sides, edges,
    strip_fields, strip_work, plane_work, circle_work, scale, strips,
):
    circle, cols = friction.shape
    tiles = circle // 8
    lane = lane_index((8, cols))
    column = lane % GROUP
    omegas = omega_list(ITERS)

    whole_column = lane_index((circle, cols)) % GROUP
    for side in range(2):
        values = []
        for field in range(3):
            own = packed[field]
            if side == 0:
                values.append(jnp.where(whole_column < HALO, packed_left[field], own))
            else:
                values.append(jnp.where(whole_column < HALO, own, packed_right[field]))
        strip_planes(strips.at[side], values[2], layers, strip_work.at[side, 0, 0])
        for c in range(2):
            for r in range(tiles):
                put_tile(strip_fields.at[0, side, c], r, values[c][rows_of(r)], tiles)
    for r in range(tiles):
        both = jnp.where(
            column == HALO - 1, strips[0, 0, rows_of(r), :], strips[1, 0, rows_of(r), :]
        )
        eta_edge[rows_of(r), :] = both

    zero = jnp.zeros((stored(circle), cols), F32)
    for end in (0, layers + 1):
        eta[end] = zero
        for half in range(2):
            for c in range(2):
                fields[half, c, end] = zero
                products[half, c, end] = zero
    covered = ice[...] > 0
    extend(friction, fr[...], above, below, 3 * layers)
    for layer in range(layers):
        slot = circle_work.at[layer % 2]
        values = eta_in[layer]
        signed = slot.at[0]
        extend(signed, jnp.where(covered, values, -values), above, below, 2 * layers + layer)
        for c in range(2):
            values = jnp.where(covered, adj[c, layer], 0.0)
            extend(slot.at[1 + c], values, above, below, c * layers + layer)
        for r in range(tiles):
            here = signed[rows_of(r), :]
            if layer == 0:
                cover[rows_of(r), :] = jnp.where(here > 0.0, 2.0, 0.0)
            e = jnp.abs(here)
            put_tile(eta.at[layer + 1], r, e, tiles)
            for c in range(2):
                f = slot[1 + c, rows_of(r), :]
                put_tile(fields.at[0, c, layer + 1], r, f, tiles)
                products[0, c, layer + 1, LEAD + 8 * r : LEAD + 8 * (r + 1), :] = e * f

    def weigh(k, slot):
        is_end = (k == 0) | (k == layers - 1)
        ends = jnp.where(is_end, 1.0, 2.0)
        lowest = jnp.where(k == layers - 1, 1.0, 0.0)
        plane = eta.at[k + 1]
        for r in range(tiles):
            e = tile_of(plane, r)
            edge = pltpu.roll(eta_edge[rows_of(r), :], cols - (GROUP * k + HALO), 1)
            e_y = lanes_before(jnp.where(lane == cols - 1, edge, e))
            e_y = e_y + lanes_after(jnp.where(lane == 0, edge, e))
            pair = inverse_pair(
                e,
                tile_of(plane, r, -1) + tile_of(plane, r, 1),
                e_y,
                tile_of(eta.at[k], r) + tile_of(eta.at[k + 2], r),
                ends,
                lowest * friction[rows_of(r), :],
                cover[rows_of(r), :],
            )
            scale[0, k, rows_of(r), :], scale[1, k, rows_of(r), :] = pair

    over_layers(layers, weigh)

    total = math.prod(omegas)
    for turn, omega in enumerate(omegas):
        final = turn == ITERS - 1
        half = turn % 2
        olds = strip_fields.at[half]
        news = strip_fields.at[1 - half]
        keep = keep_of(omega)
        if final:
            join_edges(
                edges, (strips.at[0], strips.at[1]), olds.at[0], olds.at[1], column, tiles - 1 + 1
            )
        else:
            for side in range(2):
                strip_sweep(
                    strips.at[side], olds.at[side], news.at[side], keep, strip_work.at[side]
                )
            join_sides(sides, news.at[0], news.at[1], column)

        def put(c, k, r, e, new, final=final, half=half):
            if final:
                out[c, k, rows_of(r), :] = total * new
            else:
                put_tile(fields.at[1 - half, c, k + 1], r, new, tiles)
                products[1 - half, c, k + 1, LEAD + 8 * r : LEAD + 8 * (r + 1), :] = e * new

        def sweep(k, slot, final=final, half=half, keep=keep, put=put):
            plane_sweep(
                k, lane, eta, fields.at[half], products.at[half], scale, keep,
                plane_work.at[slot], put, sides, edges if final else None,
            )

        over_layers(layers, sweep)

    flow = basal_velocity[0] * out[0, layers - 1] + basal_velocity[1] * out[1, layers - 1]
    gradient[...] = jnp.where(covered, -fr[...] * flow, 0.0)
    for i in range(2):
        for k in range(ITERS):
            carry_out[i, k] = scale[i, k]
        for k in range(3):
            carry_out[i, ITERS + k] = strips[i, k]
        for k in range(2):
            carry_out[i, ITERS + 3 + k] = eta[2 * i + k + 1, LEAD : LEAD + circle, :]


def free_sweeps(adjoint, viscosity, friction, ice_mask, edges, packed, basal_velocity):
    _, layers, rows, cols = adjoint.shape
    circle = rows + 8
    plane = (circle, cols)
    kept = (stored(circle), cols)
    stack = (layers + 2,) + kept
    return pl.pallas_call(
        functools.partial(sweep_kernel, layers),
        in_specs=vmem_specs(10),
        out_specs=vmem_specs(3),
        out_shape=[
            jax.ShapeDtypeStruct(adjoint.shape, F32),
            jax.ShapeDtypeStruct((rows, cols), F32),
            jax.ShapeDtypeStruct((2, ITERS + 5) + plane, F32),
        ],
        scratch_shapes=[
            pltpu.VMEM((2, 2) + stack, F32),
            pltpu.VMEM((2, 2) + stack, F32),
            pltpu.VMEM(stack, F32),
            pltpu.VMEM(plane, F32),
            pltpu.VMEM(plane, F32),
            pltpu.VMEM(plane, F32),
            pltpu.VMEM((2,) + plane, F32),
            pltpu.VMEM((2, 2) + plane, F32),
            pltpu.VMEM((2, 2, 2) + kept, F32),
            pltpu.VMEM((2, 2, 2) + kept, F32),
            pltpu.VMEM((UNROLL, 2, 2) + kept, F32),
            pltpu.VMEM((2, 3) + plane, F32),
            pltpu.VMEM((2, layers) + plane, F32),
            pltpu.VMEM((2, 5) + plane, F32),
        ],
        compiler_params=pltpu.CompilerParams(vmem_limit_bytes=24 << 20),
        cost_estimate=pl.CostEstimate(
            flops=200_000_000, transcendentals=0, bytes_accessed=8_000_000
        ),
        name="free_sweeps",
    )(adjoint, viscosity, friction, ice_mask, *edges, *packed, basal_velocity)


EXTRA = 12
CORNER = 16


def pack_kernel(capacity, tile_in, row_in, misfit_in, out, keys_out, counts_out,
                tile, row, misfit, slot_vector, slot, sems):
    copies = [
        pltpu.make_async_copy(source, target, sems.at[i])
        for i, (source, target) in enumerate(
            ((tile_in, tile), (row_in, row), (misfit_in, misfit))
        )
    ]
    for copy in copies:
        copy.start()
    turns, lanes = tile.shape
    devices = keys_out.shape[0]
    device = lax.broadcasted_iota(jnp.int32, (devices, lanes), 0)
    at_row = lax.broadcasted_iota(jnp.int32, (lanes, lanes), 0)
    at_lane = lax.broadcasted_iota(jnp.int32, (lanes, lanes), 1)
    earlier = jnp.where(at_row < at_lane, 1.0, 0.0).astype(BF16)
    copies[0].wait()
    seen = jnp.zeros((devices, 1), F32)
    onehots, ranks = [], []
    for turn in range(turns):
        target = tile[turn : turn + 1, :]
        onehot = jnp.where(device == target, 1.0, 0.0)
        before = jnp.dot(onehot.astype(BF16), earlier, preferred_element_type=F32) + seen
        rank = jnp.sum(onehot * before, axis=0, keepdims=True).astype(jnp.int32)
        slot_vector[turn : turn + 1, :] = target * capacity + rank
        seen = seen + jnp.sum(onehot, axis=1, keepdims=True)
        onehots.append(onehot)
        ranks.append(rank)
    copy = pltpu.make_async_copy(slot_vector, slot, sems.at[3])
    copy.start()
    counts_out[...] = jnp.broadcast_to(seen, counts_out.shape)
    copies[1].wait()
    keys = jnp.zeros((devices, lanes), F32)
    for turn in range(turns):
        named = onehots[turn] * (row[turn : turn + 1, :] + 1).astype(F32)
        place = jnp.where(at_row // 2 == ranks[turn], 1.0, 0.0).astype(BF16)
        keys = keys + lax.dot_general(
            named.astype(BF16), place, (((1,), (1,)), ((), ())), preferred_element_type=F32
        )
    keys_out[...] = keys
    copies[2].wait()
    copy.wait()

    def place_row(turn, carry):
        for i in range(lanes):
            out[slot[turn, i]] = misfit[turn * lanes + i]
        return carry

    lax.fori_loop(0, turns, place_row, 0)


def pack_blocks(misfit, block_tile, block_row, devices, capacity):
    count, _, cols = misfit.shape
    grid_shape = (count // cols, cols)
    return pl.pallas_call(
        functools.partial(pack_kernel, capacity),
        in_specs=[pl.BlockSpec(memory_space=pltpu.HBM)] * 3,
        out_specs=vmem_specs(3),
        out_shape=[
            jax.ShapeDtypeStruct((devices * capacity, 2, cols), BF16),
            jax.ShapeDtypeStruct((devices, cols), F32),
            jax.ShapeDtypeStruct((devices, cols), F32),
        ],
        scratch_shapes=[
            pltpu.VMEM(grid_shape, jnp.int32),
            pltpu.VMEM(grid_shape, jnp.int32),
            pltpu.VMEM(misfit.shape, BF16),
            pltpu.VMEM(grid_shape, jnp.int32),
            pltpu.SMEM(grid_shape, jnp.int32),
            pltpu.SemaphoreType.DMA((4,)),
        ],
        compiler_params=pltpu.CompilerParams(vmem_limit_bytes=4 << 20),
        name="pack_blocks",
    )(block_tile.reshape(grid_shape), block_row.reshape(grid_shape), misfit)


def wanted_of(keys, rows):
    odd = lax.broadcasted_iota(jnp.int32, keys.shape, 1) % 2
    return jnp.where(keys > 0.0, keys - 1.0 + odd.astype(F32) * rows, -1.0)


def halves(values):
    high = values.astype(BF16).astype(F32)
    return jnp.concatenate([high, values - high], axis=0)


CHUNKS = 4


def bundle_kernel(
    devices, across, capacity, rows, slots, keys, counts, out_hbm, upper, lower, column, out, sems
):
    lanes = slots.shape[1]
    span = 2 * capacity
    place = span + 2 * EXTRA
    at_row = lax.broadcasted_iota(jnp.int32, (span, lanes), 0).astype(F32)
    line = lax.broadcasted_iota(jnp.int32, (8, lanes), 0)
    lane = lax.broadcasted_iota(jnp.int32, (8, lanes), 1)
    ends = jnp.where(line < 4, rows - 2, 0) + (line // 2 % 2) * rows + line % 2
    ends = ends[:, :span].astype(F32)
    pick = (line == 1) & (lane == lanes - 2) | (line == 2) & (lane == lanes - 1)
    pick = pick | (line == 3) & (lane == 0) | (line == 4) & (lane == 1)
    pick = jnp.where(pick, 1.0, 0.0).astype(BF16)
    for t in range(devices):
        used = 2.0 * counts[t : t + 1, :]
        block = slots[span * t : span * (t + 1), :].astype(F32)
        block = jnp.where(at_row < used, block, 0.0).astype(BF16)
        out[place * t : place * t + span, :] = block
        wanted = wanted_of(keys[t : t + 1, :], rows)[:, :span]
        select = jnp.where(ends == wanted, 1.0, 0.0).astype(BF16)
        found = jnp.dot(select, block, preferred_element_type=F32)
        upper[t] = halves(found[:4])
        lower[t] = halves(found[4:])
        side = lax.dot_general(
            pick, block, (((1,), (1,)), ((), ())), preferred_element_type=F32
        )
        if span < lanes:
            side = jnp.concatenate([side, jnp.zeros((8, lanes - span), F32)], axis=1)
        column[t] = side
    copies = []
    zero_row = jnp.zeros((1, lanes), F32)
    zero_edge = jnp.zeros((8, lanes), F32)
    for t in range(devices):
        has_left, has_right = t % across > 0, t % across < across - 1
        has_above, has_below = t >= across, t < devices - across
        above = upper[t - across] if has_above else zero_edge
        below = lower[t + across] if has_below else zero_edge
        corner = zero_edge
        for near, there, edge, first in (
            (t - across, has_above, upper, 0),
            (t + across, has_below, lower, 8),
        ):
            if there and has_left:
                value = pltpu.roll(edge[near - 1], HALO + first, 1)
                corner = jnp.where((lane == first + 1) | (lane == first + 2), value, corner)
            if there and has_right:
                value = pltpu.roll(edge[near + 1], HALO + first, 1)
                corner = jnp.where((lane == first + 3) | (lane == first + 4), value, corner)
        corner = pltpu.roll(corner, 0, 1, stride=CORNER, stride_axis=0)
        corner = jnp.sum(corner, axis=0, keepdims=True)
        key_left = keys[t - 1 : t, :] if has_left else zero_row
        key_right = keys[t + 1 : t + 2, :] if has_right else zero_row
        left = column[t - 1, 1:3, :] if has_left else zero_edge[:2]
        right = column[t + 1, 3:5, :] if has_right else zero_edge[:2]
        head = jnp.concatenate(
            [keys[t : t + 1, :], key_left, key_right, corner, left, right], axis=0
        )
        extra = jnp.concatenate([head, above, below], axis=0).astype(BF16)
        out[place * t + span : place * (t + 1), :] = extra
        if (t + 1) % (devices // CHUNKS) == 0:
            chunk = t // (devices // CHUNKS)
            part = pl.ds(chunk * place * (devices // CHUNKS), place * (devices // CHUNKS))
            copy = pltpu.make_async_copy(out.at[part], out_hbm.at[part], sems.at[chunk])
            copy.start()
            copies.append(copy)
    for copy in copies:
        copy.wait()


def bundle_blocks(slots, keys, counts, across, capacity, rows):
    devices, cols = keys.shape
    length = devices * 2 * (capacity + EXTRA)
    edge = pltpu.VMEM((devices, 8, cols), F32)
    return pl.pallas_call(
        functools.partial(bundle_kernel, devices, across, capacity, rows),
        in_specs=vmem_specs(3),
        out_specs=pl.BlockSpec(memory_space=pltpu.HBM),
        out_shape=jax.ShapeDtypeStruct((length, cols), BF16),
        scratch_shapes=[
            edge,
            edge,
            edge,
            pltpu.VMEM((length, cols), BF16),
            pltpu.SemaphoreType.DMA((CHUNKS,)),
        ],
        compiler_params=pltpu.CompilerParams(vmem_limit_bytes=8 << 20),
        name="bundle_blocks",
    )(slots, keys, counts)


def source_of(devices, capacity, rows, got, source, beside):
    lanes = got.shape[1]
    circle = rows + 8
    span = 2 * capacity
    place = span + 2 * EXTRA
    group = max(1, lanes // span)
    at_row = lax.broadcasted_iota(jnp.int32, (2 * rows, lanes), 0).astype(F32)
    line = lax.broadcasted_iota(jnp.int32, (8, lanes), 0)
    total = jnp.zeros((2 * rows, lanes), F32)
    side = jnp.zeros((2 * rows, 8), F32)
    extra_sum = jnp.zeros((2 * EXTRA, lanes), F32)
    contract = (((1,), (1,)), ((), ()))
    pair_pick, pair_block = [], []
    for first in range(0, devices, group):
        keys, blocks = None, []
        for q in range(group):
            start = (first + q) * place
            extra = got[start + span : start + place, :].astype(F32)
            extra_sum = extra_sum + extra
            head = pltpu.roll(extra[:8], q * span, 1) if q else extra[:8]
            keys = head if keys is None else keys + head
            blocks.append(got[start : start + span, :])
        wanted = wanted_of(keys[:3], rows)
        block = blocks[0] if group == 1 else jnp.concatenate(blocks, axis=0)
        picks = [
            jnp.where(at_row == wanted[i : i + 1], 1.0, 0.0).astype(BF16) for i in range(3)
        ]
        pair_pick.append(picks[0])
        pair_block.append(block)
        if len(pair_pick) == 2:
            pick, block = jnp.concatenate(pair_pick, axis=1), jnp.concatenate(pair_block, axis=0)
            total = total + jnp.dot(pick, block, preferred_element_type=F32)
            pair_pick, pair_block = [], []
        low = jnp.where((line == 1) | (line == 2), pltpu.roll(keys, 5, 0), 0.0).astype(BF16)
        high = jnp.where((line == 3) | (line == 4), pltpu.roll(keys, 5, 0), 0.0).astype(BF16)
        pick, both = jnp.concatenate(picks[1:], axis=1), jnp.concatenate([low, high], axis=1)
        side = side + lax.dot_general(pick, both, contract, preferred_element_type=F32)
    above = extra_sum[8:12] + extra_sum[12:16]
    below = extra_sum[16:20] + extra_sum[20:24]
    lane = lax.broadcasted_iota(jnp.int32, (8, lanes), 1)
    corner = jnp.where(lane // CORNER == 7 - line, extra_sum[3:4], 0.0)
    corner = pltpu.roll(corner, lanes - 7 * CORNER, 1, stride=CORNER, stride_axis=0)
    corner = corner[:4] + corner[4:]
    corner = jnp.concatenate([corner[3 - i : 4 - i] for i in range(4)], axis=0)
    corner_below = pltpu.roll(corner, lanes - 8, 1)
    side = jnp.concatenate([side, jnp.zeros((2 * rows, lanes - 8), F32)], axis=1)
    gap = jnp.zeros((4, lanes), F32)
    for c in range(2):
        for target, inner, after, before in (
            (source, total, below, above),
            (beside, side, corner_below, corner),
        ):
            target[c, :rows, :] = inner[c * rows : (c + 1) * rows]
            target[c, rows : rows + 2, :] = after[2 * c : 2 * c + 2]
            target[c, rows + 2 : circle - 2, :] = gap
            target[c, circle - 2 : circle, :] = before[2 * c : 2 * c + 2]


def response_kernel(
    devices, capacity,
    got, scale, adj_in,
    out, source, beside, fields, products, eta, sides, edges,
    drives, strip_fields, strip_work, plane_work, strips,
):
    circle, cols = source.shape[1:]
    rows = out.shape[2]
    tiles = circle // 8
    source_of(devices, capacity, rows, got, source, beside)
    lane = lane_index((8, cols))
    column = lane % GROUP
    omegas = omega_list(ITERS)
    zero = jnp.zeros((stored(circle), cols), F32)
    top = lane < GROUP
    for side in range(2):
        for r in range(tiles):
            e = scale[side, ITERS, rows_of(r), :]
            for i in range(3):
                strips[side, i, rows_of(r), :] = scale[side, ITERS + i, rows_of(r), :]
            strips[side, 3, rows_of(r), :] = e + lanes_before(e, GROUP)
            strips[side, 4, rows_of(r), :] = e + lanes_after(e, GROUP)
    for k in range(2):
        for half in range(2):
            for c in range(2):
                fields[half, c, 0] = zero
                products[half, c, 0] = zero
                fields[half, c, 2 + half + k] = zero
                products[half, c, 2 + half + k] = zero
    eta[0] = zero
    for k in range(ITERS + 1):
        for r in range(tiles):
            put_tile(eta.at[k + 1], r, scale[k // 2, ITERS + 3 + k % 2, rows_of(r), :], tiles)

    def put_strip(turn, side, c, r, value):
        put_tile(strip_fields.at[turn % 2, side, c], r, value, tiles)

    for r in range(tiles):
        e = tile_of(eta.at[1], r)
        for c in range(2):
            drive = 0.5 * source[c, rows_of(r), :]
            source[c, rows_of(r), :] = drive
            f = scale[c, 0, rows_of(r), :] * drive
            put_tile(fields.at[0, c, 1], r, f, tiles)
            products[0, c, 1, LEAD + 8 * r : LEAD + 8 * (r + 1), :] = e * f
            own = lanes_before(drive, HALO)
            near = 0.5 * beside[c, rows_of(r), :]
            for side in range(2):
                pair = (near, own) if side == 0 else (own, near)
                both = jnp.where(top, jnp.where(column < HALO, pair[0], pair[1]), 0.0)
                drives[side, c, rows_of(r), :] = both
                put_strip(0, side, c, r, strips[side, 1 + c, rows_of(r), :] * both)

    reach = omegas[0]
    for turn in range(1, ITERS):
        final = turn == ITERS - 1
        half = turn - 1
        part = 1.0 / reach
        keep = keep_of(omegas[turn])
        olds, news = strip_fields.at[half % 2], strip_fields.at[turn % 2]
        if final:
            join_edges(
                edges, (strips.at[0], strips.at[1]), olds.at[0], olds.at[1], column, tiles
            )
        else:
            for side in range(2):
                strip_sweep(
                    strips.at[side], olds.at[side], news.at[side], keep, strip_work.at[side],
                    lambda c, r, side=side: part * drives[side, c, rows_of(r), :],
                )
            join_sides(sides, news.at[0], news.at[1], column)
        after = reach * omegas[turn]

        def put(c, k, r, e, new, final=final, turn=turn, after=after):
            if final:
                out[c, k, rows_of(r), :] = adj_in[c, k, rows_of(r), :] + after * new
            else:
                put_tile(fields.at[turn, c, k + 1], r, new, tiles)
                products[turn, c, k + 1, LEAD + 8 * r : LEAD + 8 * (r + 1), :] = e * new

        for r in range(tiles - 1 if final else tiles):
            e = tile_of(eta.at[turn + 1], r)
            for c in range(2):
                near = e * tile_of(fields.at[half, c, turn], r) + tile_of(products.at[half, c, turn], r)
                put(c, turn, r, e, scale[c, turn, rows_of(r), :] * near)
        for k in range(turn):
            drive = None
            if k == 0:
                drive = lambda c, r, part=part: part * source[c, rows_of(r), :]
            plane_sweep(
                k, lane, eta, fields.at[half], products.at[half], scale, keep,
                plane_work.at[k % 2], put, sides, edges if final else None, drive,
            )
        reach = after


def add_response(got, devices, capacity, carry, adjoint):
    circle, cols = carry.shape[2:]
    _, _, rows, _ = adjoint.shape
    plane = (circle, cols)
    kept = (stored(circle), cols)
    top = pl.BlockSpec((2, ITERS, rows, cols), lambda i: (0, 0, 0, 0))

    def whole(array):
        return pl.BlockSpec(array.shape, lambda i, n=array.ndim: (0,) * n)

    return pl.pallas_call(
        functools.partial(response_kernel, devices, capacity),
        grid=(1,),
        in_specs=[whole(got), whole(carry), top],
        out_specs=top,
        out_shape=jax.ShapeDtypeStruct(adjoint.shape, F32),
        scratch_shapes=[
            pltpu.VMEM((2,) + plane, F32),
            pltpu.VMEM((2,) + plane, F32),
            pltpu.VMEM((2, 2, ITERS + 2) + kept, F32),
            pltpu.VMEM((2, 2, ITERS + 2) + kept, F32),
            pltpu.VMEM((ITERS + 2,) + kept, F32),
            pltpu.VMEM((2,) + plane, F32),
            pltpu.VMEM((2, 2) + plane, F32),
            pltpu.VMEM((2, 2) + plane, F32),
            pltpu.VMEM((2, 2, 2) + kept, F32),
            pltpu.VMEM((2, 2, 2) + kept, F32),
            pltpu.VMEM((2, 2, 2) + kept, F32),
            pltpu.VMEM((2, 5) + plane, F32),
        ],
        input_output_aliases={2: 0},
        compiler_params=pltpu.CompilerParams(vmem_limit_bytes=12 << 20),
        name="add_response",
    )(got, carry, adjoint)


def on_device(
    adjoint_prev, viscosity, friction, basal_velocity, ice_mask, misfit, block_tile, block_row
):
    devices = lax.axis_size("gx") * lax.axis_size("gy")
    layers, rows, cols = adjoint_prev.shape[1:]
    capacity = 2 * misfit.shape[0] // devices
    assert layers > 2 * ITERS and GROUP * (layers + 1) <= cols and rows % 8 == 0
    assert devices % (cols // capacity) == 0 and 2 * capacity <= cols and cols % (2 * capacity) == 0 and misfit.shape[0] % cols == 0

    edge_low, edge_high = edge_rows(adjoint_prev, viscosity, friction, ice_mask)
    above = shift_up(edge_high, "gx")
    below = shift_down(edge_low, "gx")
    slots, keys, counts = pack_blocks(misfit, block_tile, block_row, devices, capacity)
    sent = bundle_blocks(
        slots.reshape(-1, cols), keys, counts, lax.axis_size("gy"), capacity, rows
    )
    got = lax.all_to_all(
        sent.reshape(devices, -1, cols), ("gx", "gy"), split_axis=0, concat_axis=0, tiled=True
    )
    packed = edge_columns(adjoint_prev, viscosity, friction, ice_mask, above, below)
    left = shift_up(packed, "gy")
    right = shift_down(packed, "gy")
    adjoint, gradient, carry = free_sweeps(
        adjoint_prev, viscosity, friction, ice_mask, (above, below), (packed, left, right),
        basal_velocity,
    )
    adjoint = add_response(
        got.reshape(-1, cols), devices, capacity, carry, adjoint
    )
    return (adjoint, gradient)


def solution(mesh):
    placed = (
        P(None, None, "gx", "gy"),
        P(None, "gx", "gy"),
        P("gx", "gy"),
        P(None, "gx", "gy"),
        P("gx", "gy"),
        P(("gx", "gy"), None, None),
        P(("gx", "gy"), None),
        P(("gx", "gy")),
    )

    return jax.shard_map(
        on_device,
        mesh=mesh,
        in_specs=placed,
        out_specs=(P(None, None, "gx", "gy"), P("gx", "gy")),
        check_vma=False,
    )
```
